32 devices in a mesh: groups: 2 (over x), span: 16 (over z, y, core).
Axes of the slice: x: 2, y: 2, z: 4, core: 2. Of those that a mesh axis runs over, the one named last changes fastest.
Arguments:
- queries: bfloat16 [8192, 2560], P(('groups', 'span')), parts along dimension 0, may hold values from -100 to 100
- cross_queries: bfloat16 [8192, 2560], P(('groups', 'span')), parts along dimension 0, may hold values from -100 to 100
- frame_kv: bfloat16 [8192, 5120], P(('groups', 'span')), parts along dimension 0, may hold values from -7 to 7
- sink_kv: bfloat16 [32, 64, 5120], P(('groups', 'span')), parts along dimension 0, may hold values from -5 to 5
- prompt_kv: bfloat16 [4, 512, 5120], P('groups', 'span'), parts along dimension 0, may hold values from -7 to 7
- switch: int32 [8], P('groups'), parts along dimension 0, may hold values from 0 to 4
Outputs:
- self_out: bfloat16 [8192, 2560], P(('groups', 'span')), parts along dimension 0
- cross_out: bfloat16 [8192, 2560], P(('groups', 'span')), parts along dimension 0
The draws below stay inside these ranges and needn't reach their ends.
There are 2 independent parts, one for each index of `groups`. The reference program is written for one: setup_inputs(seed, part) draws one part's arguments, and reference() takes and returns one part's arrays. A program takes and returns all parts, laid end to end along the dimension named above; each array names one. Nothing has to cross between parts.
All inputs are finite; a program needn't handle non-finite values.
Results may differ from the reference program's by a relative error of at most 0.006.
Values may be sent and summed in bfloat16 or wider, within the bound.
A program may use at most 128 MiB of HBM per device.

```python
import math
import jax
import jax.numpy as jnp
from jax import lax

HEADS = 20
HDIM = 128
FRAME = 256
WIN = 4
PTOK = 512
PROMPTS = 2
HD = 2560
STREAMS = 4
TOKENS = 4096
N_SPAN = 16


def clipped_normal(key, shape):
    return jnp.clip(jax.random.normal(key, shape, jnp.float32), -5.0, 5.0)


def frame_keys(key):
    key_rows = clipped_normal(jax.random.fold_in(key, 7), (TOKENS, HEADS * HDIM))
    return key_rows


def draw_frame_kv(key, part):
    values = clipped_normal(jax.random.fold_in(key, 8), (TOKENS, HEADS * HDIM))
    return jnp.concatenate([frame_keys(key), values], axis=1).astype(jnp.bfloat16)


def draw_queries(key, part):
    query_rows = clipped_normal(jax.random.fold_in(key, 9), (TOKENS, HEADS * HDIM))
    return query_rows.astype(jnp.bfloat16)


def draw_prompt_kv(key, part):
    stacked = []
    for prompt in range(PROMPTS):
        key_rows = clipped_normal(jax.random.fold_in(key, 20 + prompt), (PTOK, HEADS * HDIM))
        values = clipped_normal(jax.random.fold_in(key, 40 + prompt), (PTOK, HEADS * HDIM))
        stacked.append(jnp.concatenate([key_rows, values], axis=1))
    return jnp.stack(stacked, axis=0).astype(jnp.bfloat16)


def draw_cross_queries(key, part):
    query_rows = clipped_normal(jax.random.fold_in(key, 13), (TOKENS, HEADS * HDIM))
    return query_rows.astype(jnp.bfloat16)


def place_ends(entries, stream_key, smallest, largest):
    spot = [jax.random.randint(jax.random.fold_in(stream_key, axis), (), 0, length) for axis, length in enumerate(entries.shape)]
    longest = entries.shape.index(max(entries.shape))
    neighbour = spot[:longest] + [(spot[longest] + 1) % entries.shape[longest]] + spot[longest + 1:]
    return entries.at[tuple(spot)].set(smallest).at[tuple(neighbour)].set(largest)


def shard_levels(own_key, extent, cuts, smallest, high):
    loudness, own = 1.0, jax.random.fold_in(own_key, 6)
    for axis_at, shards_of in cuts:
        steps = jnp.exp(jax.random.uniform(jax.random.fold_in(own, axis_at), (shards_of,), jnp.float32, smallest / len(cuts), high / len(cuts)))
        loudness = loudness * jnp.repeat(steps, extent[axis_at] // shards_of).reshape([-1 if axis == axis_at else 1 for axis in range(len(extent))])
    return loudness


def scatter_about(rng, dims, spread, most, pieces=(), held_as=jnp.bfloat16):
    level = shard_levels(rng, dims, pieces, -0.22, 0.18) if pieces else 1.0
    result = jax.random.normal(rng, dims, jnp.float32) * spread * level
    return jnp.minimum(jnp.maximum(result, -most), most).astype(held_as)


def setup_inputs(seed: int = 0, part: int = 0) -> dict:
    keys = jax.random.split(jax.random.key(seed), 7)
    part_keys = jax.random.split(jax.random.fold_in(keys[6], part), 7)
    return {
        "queries": draw_queries(jax.random.fold_in(jax.random.fold_in(keys[6], part), 71), part),
        "cross_queries": draw_cross_queries(jax.random.fold_in(jax.random.fold_in(keys[6], part), 71), part),
        "frame_kv": draw_frame_kv(jax.random.fold_in(jax.random.fold_in(keys[6], part), 71), part),
        "sink_kv": scatter_about(part_keys[3], (N_SPAN, FRAME // WIN, 2 * HD), 1.0, 5.0, ((0, 16),)),
        "prompt_kv": draw_prompt_kv(jax.random.fold_in(jax.random.fold_in(keys[6], part), 71), part),
        "switch": place_ends(jax.random.randint(part_keys[5], (STREAMS,), 0, WIN + 1), jax.random.fold_in(part_keys[5], 1), 0, WIN).astype(jnp.int32),
    }


def softmax_blend(query_rows, key_rows, value_rows, visible):
    scores = jnp.einsum('qhd,khd->hqk', query_rows, key_rows) * (1.0 / math.sqrt(HDIM))
    if visible is not None:
        scores = jnp.where(visible[None], scores, -jnp.inf)
    row_max = lax.optimization_barrier(jnp.max(scores, axis=-1, keepdims=True))
    weights = jnp.exp(scores - row_max)
    totals = lax.optimization_barrier(jnp.sum(weights, axis=-1))
    rounded = lax.optimization_barrier(weights.astype(jnp.bfloat16)).astype(jnp.float32)
    blended = jnp.einsum('hqk,khd->qhd', rounded, value_rows)
    return (blended / jnp.transpose(totals)[:, :, None]).astype(jnp.bfloat16)

def reference(queries, cross_queries, frame_kv, sink_kv, prompt_kv, switch):
    streams = N_SPAN // WIN
    stream_queries = jnp.transpose(queries.astype(jnp.float32).reshape(WIN, streams, FRAME, HEADS, HDIM), (1, 0, 2, 3, 4)).reshape(streams, WIN * FRAME, HEADS, HDIM)
    stream_kv = jnp.transpose(frame_kv.astype(jnp.float32).reshape(WIN, streams, FRAME, 2, HEADS, HDIM), (1, 0, 2, 3, 4, 5)).reshape(streams, WIN * FRAME, 2, HEADS, HDIM)
    stream_sink = jnp.transpose(sink_kv.astype(jnp.float32).reshape(WIN, streams, FRAME // WIN, 2, HEADS, HDIM), (1, 0, 2, 3, 4, 5)).reshape(streams, FRAME, 2, HEADS, HDIM)
    key_block = jnp.concatenate([jnp.zeros((FRAME,), jnp.int32), jnp.repeat(jnp.arange(WIN, dtype=jnp.int32) + 1, FRAME)])
    query_frame = jnp.repeat(jnp.arange(WIN, dtype=jnp.int32), FRAME)
    visible = key_block[None, :] <= query_frame[:, None] + 1

    def one_stream(inputs_one):
        query_rows, kv_rows, sink_rows = inputs_one
        key_rows = jnp.concatenate([sink_rows[:, 0], kv_rows[:, 0]], axis=0)
        value_rows = jnp.concatenate([sink_rows[:, 1], kv_rows[:, 1]], axis=0)
        return softmax_blend(query_rows, key_rows, value_rows, visible).reshape(WIN * FRAME, HEADS * HDIM)
    per_stream = lax.map(one_stream, (stream_queries, stream_kv, stream_sink))
    self_out = jnp.transpose(per_stream.reshape(streams, WIN, FRAME, HEADS * HDIM), (1, 0, 2, 3)).reshape(N_SPAN * FRAME, HEADS * HDIM)
    devices = jnp.arange(N_SPAN, dtype=jnp.int32)
    window_place = devices // streams
    stream_index = devices % streams
    prompt_id = (window_place >= switch[stream_index]).astype(jnp.int32)
    frame_queries = cross_queries.astype(jnp.float32).reshape(N_SPAN, FRAME, HEADS, HDIM)
    bank = prompt_kv.astype(jnp.float32).reshape(PROMPTS, PTOK, 2, HEADS, HDIM)

    def one_frame(inputs_one):
        query_rows, chosen = inputs_one
        picked = lax.dynamic_index_in_dim(bank, chosen.astype(jnp.int32), 0, keepdims=False)
        return softmax_blend(query_rows, picked[:, 0], picked[:, 1], None).reshape(FRAME, HEADS * HDIM)
    cross_out = lax.map(one_frame, (frame_queries, prompt_id)).reshape(N_SPAN * FRAME, HEADS * HDIM)
    return (self_out, cross_out)
```

```python
import functools
import math

import jax
import jax.numpy as jnp
from jax import lax
from jax.experimental import pallas as pl
from jax.experimental.pallas import tpu as pltpu
from jax.sharding import PartitionSpec as P

HEADS = 20
HDIM = 128
WIN = 4
BUNDLE = 4
CHUNKS = HEADS // BUNDLE
LAST = CHUNKS - 1
BW = BUNDLE * HDIM
WIDTH = HEADS * HDIM
SCALE = 1.0 / math.sqrt(HDIM)
LOG2E = 1.4426950408889634
MESH = pl.DeviceIdType.MESH


def attend(query, pieces):
    scores = [
        lax.dot_general(query, keys, (((1,), (1,)), ((), ())), preferred_element_type=jnp.float32)
        for keys, _ in pieces
    ]
    peak = functools.reduce(
        jnp.maximum, [jnp.max(piece, axis=1, keepdims=True) for piece in scores]
    )
    total, blended = None, None
    for piece, (_, values) in zip(scores, pieces):
        weights = jnp.exp2((piece - peak) * (SCALE * LOG2E))
        part_sum = jnp.sum(weights, axis=1, keepdims=True)
        part = jnp.dot(weights.astype(jnp.bfloat16), values, preferred_element_type=jnp.float32)
        total = part_sum if total is None else total + part_sum
        blended = part if blended is None else blended + part
    return blended / total, peak * (SCALE * LOG2E), total


def cols(chunk, width=BW, base=0):
    return pl.ds(pl.multiple_of(base + chunk * width, 128), width)


def head_cols(head, base=0):
    return pl.ds(pl.multiple_of(base + head * HDIM, 128), HDIM)


def self_kernel(with_prompts, *refs):
    if with_prompts:
        (q_ref, kv_ref, sink_ref, prompt_ref, cq_ref, pick_ref, out_ref, cross_ref, *refs) = refs
        (bank, pr_s, pr_r, own_sem, *refs) = refs
    else:
        (q_ref, kv_ref, sink_ref, out_ref, *refs) = refs
    (kv_prev, sinks, q_in, o_send, o_recv, st_send, st_recv,
     kv_s, kv_r, q_s, q_r, s_s, s_r, o_s, o_r, st_s, st_r) = refs
    stride = lax.axis_size("span") // WIN
    me = lax.axis_index("span")
    place = me // stride
    stream = me % stride
    across = (stream + 2) % 4
    beside = stream + 1 - 2 * (stream % 2)
    rows_s = sink_ref.shape[0]
    rows = q_ref.shape[0]

    def at_place(index):
        return {"span": index * stride + stream}

    def remote(src, dst, send, recv, index, line=None):
        return pltpu.make_async_remote_copy(
            src_ref=src, dst_ref=dst, send_sem=send, recv_sem=recv,
            device_id=at_place(index) if line is None else {"span": index * stride + line},
            device_id_type=MESH,
        )

    def kv_copies(chunk):
        pairs = []
        for part in range(2):
            where = cols(chunk, BW, part * WIDTH)
            pairs.append((sink_ref.at[:, where], sinks.at[0:rows_s, where]))
        for part in range(2):
            where = cols(chunk, BW, part * WIDTH)
            pairs.append((kv_ref.at[:, where], kv_prev.at[:, where]))
        return [
            remote(src, dst, kv_s.at[i, chunk], kv_r.at[i, chunk], 1)
            for i, (src, dst) in enumerate(pairs)
        ]

    def q_copy(chunk, slot, index):
        return remote(
            q_ref.at[:, cols(chunk)], q_in.at[slot, :, cols(chunk)],
            q_s.at[slot, chunk], q_r.at[slot, chunk], index,
        )

    def q_relay(chunk):
        return remote(
            q_in.at[0, :, cols(chunk)], q_in.at[1, :, cols(chunk)],
            q_s.at[1, chunk], q_r.at[1, chunk], 1,
        )

    def sink_whole(which, index):
        where = pl.ds(which * rows_s, rows_s)
        return remote(
            sink_ref, sinks.at[where, :], s_s.at[which, 0, 0], s_r.at[which, 0, 0], index
        )

    def sink_chunk(which, chunk, index, own=False):
        copies = []
        for part in range(2):
            where = cols(chunk, BW, part * WIDTH)
            dst = sinks.at[which * rows_s : (which + 1) * rows_s, where]
            copies.append(remote(
                sink_ref.at[:, where] if own else dst, dst,
                s_s.at[which, chunk, part], s_r.at[which, chunk, part], index,
            ))
        return copies

    def lift_copies(frame):
        lane = LAST * (1 - frame)
        copies = []
        for part in range(2):
            where = cols(LAST, BW, part * WIDTH)
            src = sink_ref.at[:, where] if frame else sinks.at[0:rows_s, where]
            dst = sinks.at[frame * rows_s : (frame + 1) * rows_s, where]
            copies.append(remote(src, dst, kv_s.at[part, lane], kv_r.at[part, lane], 2))
        for part in range(2):
            where = cols(LAST, BW, part * WIDTH)
            src = (kv_ref if frame else kv_prev).at[:, where]
            dst = kv_prev.at[:, cols(lane, BW, part * WIDTH)]
            copies.append(remote(src, dst, kv_s.at[2 + part, lane], kv_r.at[2 + part, lane], 2))
        return copies

    def o_copy(chunk, slot, index):
        return remote(
            o_send.at[slot, :, cols(chunk)], o_recv.at[slot, :, cols(chunk)],
            o_s.at[slot, chunk], o_r.at[slot, chunk], index,
        )

    def st_copy(chunk, slot, index):
        return remote(
            st_send.at[slot, chunk], st_recv.at[slot, chunk],
            st_s.at[slot, chunk], st_r.at[slot, chunk], index,
        )

    def partial(slot, chunk, pieces_of, index):
        lanes = lax.broadcasted_iota(jnp.int32, (rows, 128), 1)
        stats = jnp.zeros((rows, 128), jnp.float32)
        for inner in range(BUNDLE):
            head = chunk * BUNDLE + inner
            blended, peak, total = attend(q_in[slot, :, head_cols(head)], pieces_of(head))
            o_send[slot, :, head_cols(head)] = blended.astype(jnp.bfloat16)
            stats = jnp.where(lanes == inner, peak + jnp.log2(total), stats)
        st_send[slot, chunk] = jnp.transpose(stats)[0:8]
        o_copy(chunk, slot, index).start()
        st_copy(chunk, slot, index).start()

    def drain_partial(slot, index, chunks):
        def drain(chunk, carry):
            o_copy(chunk, slot, index).wait_send()
            st_copy(chunk, slot, index).wait_send()
            return carry
        lax.fori_loop(0, chunks, drain, 0)

    def final(chunk, pieces_of, slots, index):
        owns = []
        for inner in range(BUNDLE):
            head = chunk * BUNDLE + inner
            owns.append(attend(q_ref[:, head_cols(head)], pieces_of(head)))
        levels_in = []
        for slot in slots:
            o_copy(chunk, slot, index).wait_recv()
            st_copy(chunk, slot, index).wait_recv()
            padded = jnp.concatenate(
                [st_recv[slot, chunk], jnp.zeros((120, rows), jnp.float32)], axis=0
            )
            levels_in.append(jnp.transpose(padded))
        for inner in range(BUNDLE):
            where = head_cols(chunk * BUNDLE + inner)
            blended, peak, total = owns[inner]
            if slots:
                levels = [peak + jnp.log2(total)]
                outs = [blended]
                for slot, level in zip(slots, levels_in):
                    levels.append(level[:, inner : inner + 1])
                    outs.append(o_recv[slot, :, where].astype(jnp.float32))
                top = functools.reduce(jnp.maximum, levels)
                shares = [jnp.exp2(level - top) for level in levels]
                whole = functools.reduce(jnp.add, shares)
                blended = functools.reduce(
                    jnp.add, [out * share for out, share in zip(outs, shares)]
                ) / whole
            out_ref[:, where] = blended.astype(jnp.bfloat16)

    def loop(low, high, body):
        def step(chunk, carry):
            body(chunk)
            return carry
        lax.fori_loop(low, high, step, 0)

    def pair(ref, head, low=None, high=None):
        part = slice(low, high)
        return ref[part, head_cols(head)], ref[part, head_cols(head, WIDTH)]

    def prompt_copy(kind, piece, line, index, to_line, own=False):
        return remote(
            prompt_ref if own else bank.at[piece, line], bank.at[piece, line],
            pr_s.at[kind, piece], pr_r.at[kind if kind > 1 else 0, piece], index, to_line,
        )

    def line_copies(here, piece):
        own = here == piece
        copies = []
        if piece <= here < WIN - 1:
            copies.append(prompt_copy(0, piece, stream, here + 1, stream, own))
        if 0 < here <= piece:
            copies.append(prompt_copy(1, piece, stream, here - 1, stream, own))
        copies.append(prompt_copy(2, piece, stream, here, across, own))
        copies.append(prompt_copy(3, piece, stream, here, beside, own))
        return copies

    def own_copy(here):
        return pltpu.make_async_copy(prompt_ref, bank.at[here, stream], own_sem)

    def spread(here, piece, which=slice(None)):
        if not with_prompts:
            return
        if piece != here:
            prompt_copy(0, piece, stream, here, stream).wait_recv()
        for copy in line_copies(here, piece)[which]:
            copy.start()

    def spread_across(here, pieces):
        if not with_prompts:
            return
        for piece in pieces:
            prompt_copy(2, piece, across, here, stream).wait_recv()
            prompt_copy(4, piece, across, here, beside).start()

    def cross(here):
        if not with_prompts:
            return
        own_copy(here).wait()
        for piece in range(WIN):
            prompt_copy(3, piece, beside, here, stream).wait_recv()
            prompt_copy(4, piece, 3 - stream, here, stream).wait_recv()
        pick = (place >= pick_ref[stream]).astype(jnp.int32)
        tokens = bank.shape[0] * bank.shape[1] * bank.shape[3]

        def chunk_of(chunk):
            for inner in range(BUNDLE):
                head = chunk * BUNDLE + inner
                keys = bank[:, :, pick, :, head_cols(head)].reshape(tokens, HDIM)
                values = bank[:, :, pick, :, head_cols(head, WIDTH)].reshape(tokens, HDIM)
                blended, _, _ = attend(cq_ref[:, head_cols(head)], [(keys, values)])
                cross_ref[:, head_cols(head)] = blended.astype(jnp.bfloat16)
        loop(0, CHUNKS, chunk_of)

    def drain_prompts(here):
        if not with_prompts:
            return
        for piece in range(WIN):
            for copy in line_copies(here, piece):
                copy.wait_send()
            prompt_copy(4, piece, across, here, beside).wait_send()

    barrier = pltpu.get_barrier_semaphore()
    greeted = [at_place((place + step) % WIN) for step in range(1, WIN)]
    if with_prompts:
        greeted += [{"span": place * stride + across}, {"span": place * stride + beside}]
    for other in greeted:
        pl.semaphore_signal(barrier, inc=1, device_id=other, device_id_type=MESH)
    pl.semaphore_wait(barrier, len(greeted))

    @pl.when(place == 0)
    def _():
        spread(0, 0)

        def send(chunk):
            for copy in kv_copies(chunk):
                copy.start()
        loop(0, 2, send)
        send(LAST)
        loop(2, LAST, send)
        if with_prompts:
            own_copy(0).start()
        sinks[0:rows_s, :] = sink_ref[...]
        spread(0, 1)
        spread_across(0, (0, 1))
        spread(0, 2)
        spread_across(0, (2,))
        spread(0, 3)
        spread_across(0, (3,))
        cross(0)
        sink_whole(1, 0).wait_recv()

        def ending(chunk):
            for which in (2, 3):
                for copy in sink_chunk(which, chunk, 0):
                    copy.wait_recv()
            final(chunk, lambda head: [pair(sinks, head), pair(kv_ref, head)], (), 0)
        loop(0, CHUNKS, ending)

        def drain(chunk):
            for copy in kv_copies(chunk):
                copy.wait_send()
        loop(0, CHUNKS, drain)
        drain_prompts(0)

    @pl.when(place == 1)
    def _():
        spread(1, 1)
        for copy in lift_copies(1):
            copy.start()
        sink_whole(1, 0).start()
        if with_prompts:
            own_copy(1).start()
        sinks[rows_s : 2 * rows_s, :] = sink_ref[...]

        def work(chunk):
            for copy in kv_copies(chunk):
                copy.wait_recv()
            for slot in range(2):
                q_copy(chunk, slot, 1).wait_recv()
                partial(
                    slot, chunk,
                    lambda head: [
                        pair(sinks, head, 0, 2 * rows_s), pair(kv_prev, head), pair(kv_ref, head)
                    ],
                    2 + slot,
                )

        def pass_sink(which, chunk):
            for copy in sink_chunk(which, chunk, 1):
                copy.wait_recv()
            for copy in sink_chunk(which, chunk, 0):
                copy.start()

        def lift():
            for copy in kv_copies(LAST):
                copy.wait_recv()
            for copy in lift_copies(0):
                copy.start()

        spread(1, 0)
        spread_across(1, (1, 0))

        def early(chunk):
            work(chunk)

            @pl.when(chunk == 0)
            def _():
                spread(1, 2)
                spread_across(1, (2,))

            @pl.when(chunk == 1)
            def _():
                spread(1, 3)
                lift()
                spread_across(1, (3,))
                cross(1)

            @pl.when(chunk == 2)
            def _():
                loop(0, 3, lambda piece: pass_sink(2, piece))
        loop(0, LAST, early)
        loop(3, CHUNKS, lambda piece: pass_sink(2, piece))

        def ending(chunk):
            pass_sink(3, chunk)
            final(
                chunk, lambda head: [pair(sinks, head), pair(kv_prev, head), pair(kv_ref, head)], (), 1
            )
        loop(0, CHUNKS, ending)
        sink_whole(1, 0).wait_send()

        def drain(chunk):
            for which in (2, 3):
                for copy in sink_chunk(which, chunk, 0):
                    copy.wait_send()
        loop(0, CHUNKS, drain)
        for frame in range(2):
            for copy in lift_copies(frame):
                copy.wait_send()
        for slot in range(2):
            drain_partial(slot, 2 + slot, LAST)
        drain_prompts(1)

    @pl.when(place == 2)
    def _():
        def send(chunk):
            q_copy(chunk, 0, 1).start()

        def relay(chunk):
            q_copy(chunk, 0, 2).wait_recv()
            q_relay(chunk).start()

        def work(chunk):
            partial(
                0, chunk,
                lambda head: [pair(sinks, head, 2 * rows_s, 3 * rows_s), pair(kv_ref, head)], 3,
            )

        def send_sink(which, own):
            def body(chunk):
                for copy in sink_chunk(which, chunk, 1, own):
                    copy.start()
            loop(0, CHUNKS, body)

        loop(0, 2, send)
        spread(2, 2, slice(0, 1))
        spread(2, 2, slice(2, 4))
        if with_prompts:
            own_copy(2).start()
        sinks[2 * rows_s : 3 * rows_s, :] = sink_ref[...]
        loop(0, 2, relay)
        spread(2, 2, slice(1, 2))
        loop(0, 2, work)
        spread(2, 1)
        spread_across(2, (2, 1))
        spread(2, 3)

        def forward(chunk):
            send(chunk)
            relay(chunk)
        loop(2, LAST, forward)
        send_sink(2, True)
        loop(2, LAST, work)
        spread_across(2, (3,))
        spread(2, 0)
        sink_whole(3, 2).wait_recv()
        send_sink(3, False)
        spread_across(2, (0,))
        cross(2)

        def ending(chunk):
            final(
                chunk,
                lambda head: [pair(sinks, head, 2 * rows_s, 4 * rows_s), pair(kv_ref, head)], (0,), 2,
            )
        loop(0, 2, ending)
        for frame in (1, 0):
            for copy in lift_copies(frame):
                copy.wait_recv()
        q_copy(LAST, 0, 2).wait_recv()

        def lifted(head, high):
            return [
                pair(sinks, head, 0, high), pair(kv_prev, head),
                pair(kv_prev, head - LAST * BUNDLE), pair(kv_ref, head),
            ]
        partial(0, LAST, lambda head: lifted(head, 3 * rows_s), 3)
        final(LAST, lambda head: lifted(head, 4 * rows_s), (), 2)
        loop(2, LAST, ending)

        def drain(chunk):
            for which in (2, 3):
                for copy in sink_chunk(which, chunk, 1, which == 2):
                    copy.wait_send()
        loop(0, CHUNKS, drain)
        loop(0, LAST, lambda chunk: q_copy(chunk, 0, 1).wait_send())
        loop(0, LAST, lambda chunk: q_relay(chunk).wait_send())
        drain_partial(0, 3, CHUNKS)
        drain_prompts(2)

    @pl.when(place == 3)
    def _():
        loop(0, 2, lambda chunk: q_copy(chunk, 0, 2).start())
        spread(3, 3)
        loop(2, CHUNKS, lambda chunk: q_copy(chunk, 0, 2).start())
        sink_whole(3, 2).start()
        if with_prompts:
            own_copy(3).start()
        spread(3, 2)
        spread_across(3, (3, 2))
        spread(3, 1)
        spread_across(3, (1,))
        spread(3, 0)
        spread_across(3, (0,))
        cross(3)

        def ending(chunk, slots=(0, 1)):
            final(chunk, lambda head: [pair(sink_ref, head), pair(kv_ref, head)], slots, 3)
        loop(0, 2, ending)
        ending(LAST, (0,))
        loop(2, LAST, ending)
        sink_whole(3, 2).wait_send()
        loop(0, CHUNKS, lambda chunk: q_copy(chunk, 0, 2).wait_send())
        drain_prompts(3)


def self_attention(queries, frame_kv, own_sink, prompts=None):
    rows = queries.shape[0]
    vmem = pl.BlockSpec(memory_space=pltpu.VMEM)
    dma = pltpu.SemaphoreType.DMA
    operands = [queries, frame_kv, own_sink]
    in_specs = [vmem] * 3
    outs = [jax.ShapeDtypeStruct((rows, WIDTH), jnp.bfloat16)]
    scratch = []
    if prompts is not None:
        operands += prompts
        in_specs += [vmem, vmem, pl.BlockSpec(memory_space=pltpu.SMEM)]
        outs = outs * 2
        scratch = [
            pltpu.VMEM((WIN, lax.axis_size("span") // WIN) + prompts[0].shape, jnp.bfloat16),
            dma((5, WIN)), dma((5, WIN)), dma,
        ]
    return pl.pallas_call(
        functools.partial(self_kernel, prompts is not None),
        out_shape=outs,
        in_specs=in_specs,
        out_specs=[vmem] * len(outs),
        scratch_shapes=scratch + [
            pltpu.VMEM((rows, 2 * WIDTH), jnp.bfloat16),
            pltpu.VMEM((WIN * own_sink.shape[0], 2 * WIDTH), jnp.bfloat16),
            pltpu.VMEM((2, rows, WIDTH), jnp.bfloat16),
            pltpu.VMEM((2, rows, WIDTH), jnp.bfloat16),
            pltpu.VMEM((2, rows, WIDTH), jnp.bfloat16),
            pltpu.VMEM((2, CHUNKS, 8, rows), jnp.float32),
            pltpu.VMEM((2, CHUNKS, 8, rows), jnp.float32),
            dma((4, CHUNKS)), dma((4, CHUNKS)),
            dma((2, CHUNKS)), dma((2, CHUNKS)),
            dma((WIN, CHUNKS, 2)), dma((WIN, CHUNKS, 2)),
            dma((2, CHUNKS)), dma((2, CHUNKS)),
            dma((2, CHUNKS)), dma((2, CHUNKS)),
        ],
        compiler_params=pltpu.CompilerParams(
            collective_id=0, has_side_effects=True, vmem_limit_bytes=60 * 1024 * 1024
        ),
    )(*operands)


def cross_kernel(pick_ref, q_ref, k_ref, v_ref, out_ref):
    for inner in range(BUNDLE):
        where = slice(inner * HDIM, (inner + 1) * HDIM)
        blended, _, _ = attend(q_ref[:, where], [(k_ref[0, :, where], v_ref[0, :, where])])
        out_ref[:, where] = blended.astype(jnp.bfloat16)


def cross_attention(cross_queries, prompts, pick):
    rows = cross_queries.shape[0]
    tokens = prompts.shape[1]
    return pl.pallas_call(
        cross_kernel,
        out_shape=jax.ShapeDtypeStruct((rows, WIDTH), jnp.bfloat16),
        grid_spec=pltpu.PrefetchScalarGridSpec(
            num_scalar_prefetch=1,
            grid=(CHUNKS,),
            in_specs=[
                pl.BlockSpec((rows, BW), lambda c, pick: (0, c)),
                pl.BlockSpec((1, tokens, BW), lambda c, pick: (pick[0], 0, c)),
                pl.BlockSpec((1, tokens, BW), lambda c, pick: (pick[0], 0, CHUNKS + c)),
            ],
            out_specs=pl.BlockSpec((rows, BW), lambda c, pick: (0, c)),
        ),
    )(pick.reshape(1), cross_queries, prompts, prompts)


def shards(queries, cross_queries, frame_kv, sink_kv, prompt_kv, switch):
    stream_count = lax.axis_size("span") // WIN
    device = lax.axis_index("span")
    place = device // stream_count
    stream_of = device % stream_count
    own_sink = sink_kv.reshape(sink_kv.shape[1], sink_kv.shape[2])
    if stream_count == 4 and prompt_kv.shape[1] % 16 == 0:
        return tuple(
            self_attention(queries, frame_kv, own_sink, [prompt_kv, cross_queries, switch])
        )
    stream_ids = jnp.arange(switch.shape[0], dtype=jnp.int32)
    switch_at = jnp.sum(jnp.where(stream_ids == stream_of, switch, 0))
    pick = (place >= switch_at).astype(jnp.int32)
    prompts = lax.all_gather(prompt_kv, "span", axis=1, tiled=True)
    (self_out,) = self_attention(queries, frame_kv, own_sink)
    cross_out = cross_attention(cross_queries, prompts, pick)
    return (self_out, cross_out)


def solution(mesh):
    in_specs = (
        P(("groups", "span"), None),
        P(("groups", "span"), None),
        P(("groups", "span"), None),
        P(("groups", "span"), None, None),
        P("groups", "span", None),
        P("groups"),
    )
    out_specs = (P(("groups", "span"), None), P(("groups", "span"), None))
    return jax.shard_map(shards, mesh=mesh, in_specs=in_specs, out_specs=out_specs, check_vma=False)
```

```python
import functools
import math

import jax
import jax.numpy as jnp
from jax import lax
from jax.experimental import pallas as pl
from jax.experimental.pallas import tpu as pltpu
from jax.sharding import PartitionSpec as P

HEADS = 20
HDIM = 128
WIN = 4
BUNDLE = 4
CHUNKS = HEADS // BUNDLE
LAST = CHUNKS - 1
BW = BUNDLE * HDIM
WIDTH = HEADS * HDIM
SCALE = 1.0 / math.sqrt(HDIM)
LOG2E = 1.4426950408889634
MESH = pl.DeviceIdType.MESH


def attend(query, pieces):
    scores = [
        lax.dot_general(query, keys, (((1,), (1,)), ((), ())), preferred_element_type=jnp.float32)
        for keys, _ in pieces
    ]
    peak = functools.reduce(
        jnp.maximum, [jnp.max(piece, axis=1, keepdims=True) for piece in scores]
    )
    total, blended = None, None
    for piece, (_, values) in zip(scores, pieces):
        weights = jnp.exp2((piece - peak) * (SCALE * LOG2E))
        part_sum = jnp.sum(weights, axis=1, keepdims=True)
        part = jnp.dot(weights.astype(jnp.bfloat16), values, preferred_element_type=jnp.float32)
        total = part_sum if total is None else total + part_sum
        blended = part if blended is None else blended + part
    return blended / total, peak * (SCALE * LOG2E), total


def cols(chunk, width=BW, base=0):
    return pl.ds(pl.multiple_of(base + chunk * width, 128), width)


def head_cols(head, base=0):
    return pl.ds(pl.multiple_of(base + head * HDIM, 128), HDIM)


def self_kernel(with_prompts, *refs):
    if with_prompts:
        (q_hbm, kv_hbm, sink_hbm, prompt_hbm, cq_hbm, pick_ref, out_ref, cross_ref, *refs) = refs
        (bank, cq_ref, pr_s, pr_r, *refs) = refs
    else:
        (q_hbm, kv_hbm, sink_hbm, out_ref, *refs) = refs
    (q_ref, kv_ref, own_out, own_level, load_sem, kv_prev, sinks, q_in, o_send, o_recv, st_send, st_recv,
     kv_s, kv_r, q_s, q_r, s_s, s_r, o_s, o_r, st_s, st_r) = refs
    stride = lax.axis_size("span") // WIN
    me = lax.axis_index("span")
    place = me // stride
    stream = me % stride
    across = (stream + 2) % 4
    beside = stream + 1 - 2 * (stream % 2)
    rows_s = sink_hbm.shape[0]
    rows = q_ref.shape[0]
    mine = pl.ds(pl.multiple_of(place * rows_s, rows_s), rows_s)

    loads = {
        "sink": pltpu.make_async_copy(sink_hbm, sinks.at[mine, :], load_sem.at[0]),
        "q": pltpu.make_async_copy(q_hbm, q_ref, load_sem.at[1]),
        "kv": pltpu.make_async_copy(kv_hbm, kv_ref, load_sem.at[2]),
    }
    if with_prompts:
        loads["prompt"] = pltpu.make_async_copy(
            prompt_hbm, bank.at[place, stream], load_sem.at[3]
        )
        loads["cq"] = pltpu.make_async_copy(cq_hbm, cq_ref, load_sem.at[4])

    def load(*names):
        for name in names:
            if name in loads:
                loads[name].start()

    def loaded(*names):
        for name in names:
            if name in loads:
                loads[name].wait()

    def at_place(index):
        return {"span": index * stride + stream}

    def remote(src, dst, send, recv, index, line=None):
        return pltpu.make_async_remote_copy(
            src_ref=src, dst_ref=dst, send_sem=send, recv_sem=recv,
            device_id=at_place(index) if line is None else {"span": index * stride + line},
            device_id_type=MESH,
        )

    def kv_copies(chunk):
        pairs = []
        for part in range(2):
            where = cols(chunk, BW, part * WIDTH)
            pairs.append((sinks.at[0:rows_s, where], sinks.at[0:rows_s, where]))
        for part in range(2):
            where = cols(chunk, BW, part * WIDTH)
            pairs.append((kv_ref.at[:, where], kv_prev.at[:, where]))
        return [
            remote(src, dst, kv_s.at[i, chunk], kv_r.at[i, chunk], 1)
            for i, (src, dst) in enumerate(pairs)
        ]

    def q_copy(chunk, slot, index):
        return remote(
            q_ref.at[:, cols(chunk)], q_in.at[slot, :, cols(chunk)],
            q_s.at[slot, chunk], q_r.at[slot, chunk], index,
        )

    def q_relay(chunk):
        return remote(
            q_in.at[0, :, cols(chunk)], q_in.at[1, :, cols(chunk)],
            q_s.at[1, chunk], q_r.at[1, chunk], 1,
        )

    def sink_whole(which, index):
        where = sinks.at[which * rows_s : (which + 1) * rows_s, :]
        return remote(where, where, s_s.at[which, 0, 0], s_r.at[which, 0, 0], index)

    def sink_chunk(which, chunk, index):
        copies = []
        for part in range(2):
            where = cols(chunk, BW, part * WIDTH)
            piece = sinks.at[which * rows_s : (which + 1) * rows_s, where]
            copies.append(remote(
                piece, piece, s_s.at[which, chunk, part], s_r.at[which, chunk, part], index
            ))
        return copies

    def lift_copies(frame):
        lane = LAST * (1 - frame)
        copies = []
        for part in range(2):
            where = cols(LAST, BW, part * WIDTH)
            piece = sinks.at[frame * rows_s : (frame + 1) * rows_s, where]
            copies.append(remote(piece, piece, kv_s.at[part, lane], kv_r.at[part, lane], 2))
        for part in range(2):
            where = cols(LAST, BW, part * WIDTH)
            src = (kv_ref if frame else kv_prev).at[:, where]
            dst = kv_prev.at[:, cols(lane, BW, part * WIDTH)]
            copies.append(remote(src, dst, kv_s.at[2 + part, lane], kv_r.at[2 + part, lane], 2))
        return copies

    def o_copy(chunk, slot, index):
        return remote(
            o_send.at[slot, :, cols(chunk)], o_recv.at[slot, :, cols(chunk)],
            o_s.at[slot, chunk], o_r.at[slot, chunk], index,
        )

    def st_copy(chunk, slot, index):
        return remote(
            st_send.at[slot, chunk], st_recv.at[slot, chunk],
            st_s.at[slot, chunk], st_r.at[slot, chunk], index,
        )

    def partial(slot, chunk, pieces_of, index):
        lanes = lax.broadcasted_iota(jnp.int32, (rows, 128), 1)
        stats = jnp.zeros((rows, 128), jnp.float32)
        for inner in range(BUNDLE):
            head = chunk * BUNDLE + inner
            blended, peak, total = attend(q_in[slot, :, head_cols(head)], pieces_of(head))
            o_send[slot, :, head_cols(head)] = blended.astype(jnp.bfloat16)
            stats = jnp.where(lanes == inner, peak + jnp.log2(total), stats)
        st_send[slot, chunk] = jnp.transpose(stats)[0:8]
        o_copy(chunk, slot, index).start()
        st_copy(chunk, slot, index).start()

    def drain_partial(slot, index, chunks):
        def drain(chunk, carry):
            o_copy(chunk, slot, index).wait_send()
            st_copy(chunk, slot, index).wait_send()
            return carry
        lax.fori_loop(0, chunks, drain, 0)

    def own_part(chunk, pieces_of):
        lanes = lax.broadcasted_iota(jnp.int32, (rows, 128), 1)
        stats = jnp.zeros((rows, 128), jnp.float32)
        for inner in range(BUNDLE):
            head = chunk * BUNDLE + inner
            blended, peak, total = attend(q_ref[:, head_cols(head)], pieces_of(head))
            own_out[:, head_cols(head)] = blended
            stats = jnp.where(lanes == inner, peak + jnp.log2(total), stats)
        own_level[chunk] = stats

    def final(chunk, pieces_of, slots, index, own=True):
        levels_in = [own_level[chunk]] if own else []
        for slot in slots:
            o_copy(chunk, slot, index).wait_recv()
            st_copy(chunk, slot, index).wait_recv()
            padded = jnp.concatenate(
                [st_recv[slot, chunk], jnp.zeros((120, rows), jnp.float32)], axis=0
            )
            levels_in.append(jnp.transpose(padded))
        for inner in range(BUNDLE):
            head = chunk * BUNDLE + inner
            where = head_cols(head)
            outs = [own_out[:, where]] if own else []
            outs += [o_recv[slot, :, where].astype(jnp.float32) for slot in slots]
            levels = [level[:, inner : inner + 1] for level in levels_in]
            if pieces_of is not None:
                blended, peak, total = attend(q_ref[:, where], pieces_of(head))
                outs.append(blended)
                levels.append(peak + jnp.log2(total))
            if len(outs) > 1:
                top = functools.reduce(jnp.maximum, levels)
                shares = [jnp.exp2(level - top) for level in levels]
                whole = functools.reduce(jnp.add, shares)
                blended = functools.reduce(
                    jnp.add, [out * share for out, share in zip(outs, shares)]
                ) / whole
            else:
                blended = outs[0]
            out_ref[:, where] = blended.astype(jnp.bfloat16)

    def loop(low, high, body):
        def step(chunk, carry):
            body(chunk)
            return carry
        lax.fori_loop(low, high, step, 0)

    def pair(ref, head, low=None, high=None):
        part = slice(low, high)
        return ref[part, head_cols(head)], ref[part, head_cols(head, WIDTH)]

    def prompt_copy(kind, piece, line, index, to_line):
        return remote(
            bank.at[piece, line], bank.at[piece, line],
            pr_s.at[kind, piece], pr_r.at[kind if kind > 1 else 0, piece], index, to_line,
        )

    def line_copies(here, piece, kinds=(0, 1, 2, 3)):
        copies = []
        if 0 in kinds and piece <= here < WIN - 1:
            copies.append(prompt_copy(0, piece, stream, here + 1, stream))
        if 1 in kinds and 0 < here <= piece:
            copies.append(prompt_copy(1, piece, stream, here - 1, stream))
        if 2 in kinds:
            copies.append(prompt_copy(2, piece, stream, here, across))
        if 3 in kinds:
            copies.append(prompt_copy(3, piece, stream, here, beside))
        return copies

    def spread(here, piece, kinds=(0, 1, 2, 3)):
        if not with_prompts:
            return
        if piece != here:
            prompt_copy(0, piece, stream, here, stream).wait_recv()
        for copy in line_copies(here, piece, kinds):
            copy.start()

    def spread_across(here, pieces):
        if not with_prompts:
            return
        for piece in pieces:
            prompt_copy(2, piece, across, here, stream).wait_recv()
            prompt_copy(4, piece, across, here, beside).start()

    def cross(here):
        if not with_prompts:
            return
        loaded("cq")
        for piece in range(WIN):
            prompt_copy(3, piece, beside, here, stream).wait_recv()
            prompt_copy(4, piece, 3 - stream, here, stream).wait_recv()
        pick = (place >= pick_ref[stream]).astype(jnp.int32)
        tokens = bank.shape[0] * bank.shape[1] * bank.shape[3]

        def chunk_of(chunk):
            for inner in range(BUNDLE):
                head = chunk * BUNDLE + inner
                keys = bank[:, :, pick, :, head_cols(head)].reshape(tokens, HDIM)
                values = bank[:, :, pick, :, head_cols(head, WIDTH)].reshape(tokens, HDIM)
                blended, _, _ = attend(cq_ref[:, head_cols(head)], [(keys, values)])
                cross_ref[:, head_cols(head)] = blended.astype(jnp.bfloat16)
        loop(0, CHUNKS, chunk_of)

    def drain_prompts(here):
        if not with_prompts:
            return
        for piece in range(WIN):
            for copy in line_copies(here, piece):
                copy.wait_send()
            prompt_copy(4, piece, across, here, beside).wait_send()

    barrier = pltpu.get_barrier_semaphore()
    greeted = [at_place((place + step) % WIN) for step in range(1, WIN)]
    if with_prompts:
        greeted += [{"span": place * stride + across}, {"span": place * stride + beside}]
    for other in greeted:
        pl.semaphore_signal(barrier, inc=1, device_id=other, device_id_type=MESH)
    load("q", "prompt", "sink", "kv", "cq")
    pl.semaphore_wait(barrier, len(greeted))

    @pl.when(place == 0)
    def _():
        loaded("prompt")
        spread(0, 0)
        loaded("sink", "kv")

        def send(chunk):
            for copy in kv_copies(chunk):
                copy.start()
        loop(0, 2, send)
        send(LAST)
        loop(2, LAST, send)
        spread(0, 1)
        spread_across(0, (0, 1))
        loaded("q")
        sink_whole(1, 0).wait_recv()
        loop(0, CHUNKS, lambda chunk: own_part(
            chunk, lambda head: [pair(sinks, head, 0, 2 * rows_s), pair(kv_ref, head)]
        ))
        spread(0, 2)
        spread_across(0, (2,))
        spread(0, 3)
        spread_across(0, (3,))
        cross(0)

        def ending(chunk):
            for which in (2, 3):
                for copy in sink_chunk(which, chunk, 0):
                    copy.wait_recv()
            final(chunk, lambda head: [pair(sinks, head, 2 * rows_s, 4 * rows_s)], (), 0)
        loop(0, CHUNKS, ending)

        def drain(chunk):
            for copy in kv_copies(chunk):
                copy.wait_send()
        loop(0, CHUNKS, drain)
        drain_prompts(0)

    @pl.when(place == 1)
    def _():
        loaded("prompt")
        spread(1, 1)
        loaded("sink", "kv")
        for copy in lift_copies(1):
            copy.start()
        sink_whole(1, 0).start()

        def work(chunk):
            for copy in kv_copies(chunk):
                copy.wait_recv()
            for slot in range(2):
                q_copy(chunk, slot, 1).wait_recv()
                partial(
                    slot, chunk,
                    lambda head: [
                        pair(sinks, head, 0, 2 * rows_s), pair(kv_prev, head), pair(kv_ref, head)
                    ],
                    2 + slot,
                )

        def own(chunk):
            own_part(chunk, lambda head: [
                pair(sinks, head, 0, 2 * rows_s), pair(kv_prev, head), pair(kv_ref, head)
            ])

        def pass_sink(which, chunk):
            for copy in sink_chunk(which, chunk, 1):
                copy.wait_recv()
            for copy in sink_chunk(which, chunk, 0):
                copy.start()

        def lift():
            for copy in kv_copies(LAST):
                copy.wait_recv()
            for copy in lift_copies(0):
                copy.start()

        spread(1, 0)
        spread_across(1, (1, 0))
        loaded("q")

        def early(chunk):
            work(chunk)

            @pl.when(chunk == 2)
            def _():
                loop(2, CHUNKS, lambda piece: pass_sink(2, piece))
            own(chunk)

            @pl.when(chunk == 0)
            def _():
                spread(1, 2)
                spread_across(1, (2,))

            @pl.when(chunk == 1)
            def _():
                spread(1, 3)
                lift()
                spread_across(1, (3,))
                own(LAST)
                cross(1)
                loop(0, 2, lambda piece: pass_sink(2, piece))
        loop(0, LAST, early)

        def ending(chunk):
            pass_sink(3, chunk)
            final(chunk, lambda head: [pair(sinks, head, 2 * rows_s, 4 * rows_s)], (), 1)
        loop(0, CHUNKS, ending)
        sink_whole(1, 0).wait_send()

        def drain(chunk):
            for which in (2, 3):
                for copy in sink_chunk(which, chunk, 0):
                    copy.wait_send()
        loop(0, CHUNKS, drain)
        for frame in range(2):
            for copy in lift_copies(frame):
                copy.wait_send()
        for slot in range(2):
            drain_partial(slot, 2 + slot, LAST)
        drain_prompts(1)

    @pl.when(place == 2)
    def _():
        def send(chunk):
            q_copy(chunk, 0, 1).start()

        def relay(chunk):
            q_copy(chunk, 0, 2).wait_recv()
            q_relay(chunk).start()

        def work(chunk):
            partial(
                0, chunk,
                lambda head: [pair(sinks, head, 2 * rows_s, 3 * rows_s), pair(kv_ref, head)], 3,
            )

        def send_sink(which):
            def body(chunk):
                for copy in sink_chunk(which, chunk, 1):
                    copy.start()
            loop(0, CHUNKS, body)

        loaded("q")
        loop(0, 2, send)
        loaded("prompt")
        spread(2, 2, (0, 2, 3))
        loop(0, 2, relay)
        spread(2, 2, (1,))
        loaded("sink", "kv")
        loop(0, 2, work)
        spread(2, 1)
        spread_across(2, (2, 1))
        spread(2, 3)

        def forward(chunk):
            send(chunk)
            relay(chunk)
        loop(2, 3, forward)
        send_sink(2)
        loop(3, LAST, forward)
        loop(2, LAST, work)
        spread_across(2, (3,))
        spread(2, 0)
        sink_whole(3, 2).wait_recv()
        send_sink(3)
        spread_across(2, (0,))
        loop(0, LAST, lambda chunk: own_part(
            chunk, lambda head: [pair(sinks, head, 2 * rows_s, 4 * rows_s), pair(kv_ref, head)]
        ))
        cross(2)

        def ending(chunk):
            final(chunk, None, (0,), 2)
        loop(0, 2, ending)
        for frame in (1, 0):
            for copy in lift_copies(frame):
                copy.wait_recv()
        q_copy(LAST, 0, 2).wait_recv()

        def lifted(head, high):
            return [
                pair(sinks, head, 0, high), pair(kv_prev, head),
                pair(kv_prev, head - LAST * BUNDLE), pair(kv_ref, head),
            ]
        partial(0, LAST, lambda head: lifted(head, 3 * rows_s), 3)
        final(LAST, lambda head: lifted(head, 4 * rows_s), (), 2, False)
        loop(2, LAST, ending)

        def drain(chunk):
            for which in (2, 3):
                for copy in sink_chunk(which, chunk, 1):
                    copy.wait_send()
        loop(0, CHUNKS, drain)
        loop(0, LAST, lambda chunk: q_copy(chunk, 0, 1).wait_send())
        loop(0, LAST, lambda chunk: q_relay(chunk).wait_send())
        drain_partial(0, 3, CHUNKS)
        drain_prompts(2)

    @pl.when(place == 3)
    def _():
        loaded("q")
        loop(0, 2, lambda chunk: q_copy(chunk, 0, 2).start())
        loaded("prompt")
        spread(3, 3)
        loop(2, CHUNKS, lambda chunk: q_copy(chunk, 0, 2).start())
        loaded("sink")
        sink_whole(3, 2).start()
        loaded("kv")
        loop(0, CHUNKS, lambda chunk: own_part(
            chunk,
            lambda head: [pair(sinks, head, 3 * rows_s, 4 * rows_s), pair(kv_ref, head)],
        ))
        spread(3, 2)
        spread_across(3, (3, 2))
        spread(3, 1)
        spread_across(3, (1,))
        spread(3, 0)
        spread_across(3, (0,))
        cross(3)

        def ending(chunk, slots=(0, 1)):
            final(chunk, None, slots, 3)
        loop(0, 2, ending)
        ending(LAST, (0,))
        loop(2, LAST, ending)
        sink_whole(3, 2).wait_send()
        loop(0, CHUNKS, lambda chunk: q_copy(chunk, 0, 2).wait_send())
        drain_prompts(3)


def self_attention(queries, frame_kv, own_sink, prompts=None):
    rows = queries.shape[0]
    vmem = pl.BlockSpec(memory_space=pltpu.VMEM)
    hbm = pl.BlockSpec(memory_space=pltpu.HBM)
    dma = pltpu.SemaphoreType.DMA
    operands = [queries, frame_kv, own_sink]
    in_specs = [hbm] * 3
    outs = [jax.ShapeDtypeStruct((rows, WIDTH), jnp.bfloat16)]
    scratch = []
    if prompts is not None:
        operands += prompts
        in_specs += [hbm, hbm, pl.BlockSpec(memory_space=pltpu.SMEM)]
        outs = outs * 2
        scratch = [
            pltpu.VMEM((WIN, lax.axis_size("span") // WIN) + prompts[0].shape, jnp.bfloat16),
            pltpu.VMEM((rows, WIDTH), jnp.bfloat16),
            dma((5, WIN)), dma((5, WIN)),
        ]
    return pl.pallas_call(
        functools.partial(self_kernel, prompts is not None),
        out_shape=outs,
        in_specs=in_specs,
        out_specs=[vmem] * len(outs),
        scratch_shapes=scratch + [
            pltpu.VMEM((rows, WIDTH), jnp.bfloat16),
            pltpu.VMEM((rows, 2 * WIDTH), jnp.bfloat16),
            pltpu.VMEM((rows, WIDTH), jnp.float32),
            pltpu.VMEM((CHUNKS, rows, 128), jnp.float32),
            dma((5,)),
            pltpu.VMEM((rows, 2 * WIDTH), jnp.bfloat16),
            pltpu.VMEM((WIN * own_sink.shape[0], 2 * WIDTH), jnp.bfloat16),
            pltpu.VMEM((2, rows, WIDTH), jnp.bfloat16),
            pltpu.VMEM((2, rows, WIDTH), jnp.bfloat16),
            pltpu.VMEM((2, rows, WIDTH), jnp.bfloat16),
            pltpu.VMEM((2, CHUNKS, 8, rows), jnp.float32),
            pltpu.VMEM((2, CHUNKS, 8, rows), jnp.float32),
            dma((4, CHUNKS)), dma((4, CHUNKS)),
            dma((2, CHUNKS)), dma((2, CHUNKS)),
            dma((WIN, CHUNKS, 2)), dma((WIN, CHUNKS, 2)),
            dma((2, CHUNKS)), dma((2, CHUNKS)),
            dma((2, CHUNKS)), dma((2, CHUNKS)),
        ],
        compiler_params=pltpu.CompilerParams(
            collective_id=0, has_side_effects=True, vmem_limit_bytes=48 * 1024 * 1024
        ),
    )(*[pltpu.with_memory_space_constraint(x, pltpu.HBM) for x in operands])


def cross_kernel(pick_ref, q_ref, k_ref, v_ref, out_ref):
    for inner in range(BUNDLE):
        where = slice(inner * HDIM, (inner + 1) * HDIM)
        blended, _, _ = attend(q_ref[:, where], [(k_ref[0, :, where], v_ref[0, :, where])])
        out_ref[:, where] = blended.astype(jnp.bfloat16)


def cross_attention(cross_queries, prompts, pick):
    rows = cross_queries.shape[0]
    tokens = prompts.shape[1]
    return pl.pallas_call(
        cross_kernel,
        out_shape=jax.ShapeDtypeStruct((rows, WIDTH), jnp.bfloat16),
        grid_spec=pltpu.PrefetchScalarGridSpec(
            num_scalar_prefetch=1,
            grid=(CHUNKS,),
            in_specs=[
                pl.BlockSpec((rows, BW), lambda c, pick: (0, c)),
                pl.BlockSpec((1, tokens, BW), lambda c, pick: (pick[0], 0, c)),
                pl.BlockSpec((1, tokens, BW), lambda c, pick: (pick[0], 0, CHUNKS + c)),
            ],
            out_specs=pl.BlockSpec((rows, BW), lambda c, pick: (0, c)),
        ),
    )(pick.reshape(1), cross_queries, prompts, prompts)


def shards(queries, cross_queries, frame_kv, sink_kv, prompt_kv, switch):
    stream_count = lax.axis_size("span") // WIN
    device = lax.axis_index("span")
    place = device // stream_count
    stream_of = device % stream_count
    own_sink = sink_kv.reshape(sink_kv.shape[1], sink_kv.shape[2])
    if stream_count == 4 and prompt_kv.shape[1] % 16 == 0:
        return tuple(
            self_attention(queries, frame_kv, own_sink, [prompt_kv, cross_queries, switch])
        )
    stream_ids = jnp.arange(switch.shape[0], dtype=jnp.int32)
    switch_at = jnp.sum(jnp.where(stream_ids == stream_of, switch, 0))
    pick = (place >= switch_at).astype(jnp.int32)
    prompts = lax.all_gather(prompt_kv, "span", axis=1, tiled=True)
    (self_out,) = self_attention(queries, frame_kv, own_sink)
    cross_out = cross_attention(cross_queries, prompts, pick)
    return (self_out, cross_out)


def solution(mesh):
    in_specs = (
        P(("groups", "span"), None),
        P(("groups", "span"), None),
        P(("groups", "span"), None),
        P(("groups", "span"), None, None),
        P("groups", "span", None),
        P("groups"),
    )
    out_specs = (P(("groups", "span"), None), P(("groups", "span"), None))
    return jax.shard_map(shards, mesh=mesh, in_specs=in_specs, out_specs=out_specs, check_vma=False)
```

```python
import functools
import math

import jax
import jax.numpy as jnp
from jax import lax
from jax.experimental import pallas as pl
from jax.experimental.pallas import tpu as pltpu
from jax.sharding import PartitionSpec as P

HEADS = 20
HDIM = 128
WIN = 4
BUNDLE = 4
CHUNKS = HEADS // BUNDLE
LAST = CHUNKS - 1
STORES = 4
BW = BUNDLE * HDIM
WIDTH = HEADS * HDIM
SCALE = 1.0 / math.sqrt(HDIM)
LOG2E = 1.4426950408889634
MESH = pl.DeviceIdType.MESH


def attend(query, pieces):
    scores = [
        lax.dot_general(query, keys, (((1,), (1,)), ((), ())), preferred_element_type=jnp.float32)
        for keys, _ in pieces
    ]
    peak = functools.reduce(
        jnp.maximum, [jnp.max(piece, axis=1, keepdims=True) for piece in scores]
    )
    total, blended = None, None
    for piece, (_, values) in zip(scores, pieces):
        weights = jnp.exp2((piece - peak) * (SCALE * LOG2E))
        part_sum = jnp.sum(weights, axis=1, keepdims=True)
        part = jnp.dot(weights.astype(jnp.bfloat16), values, preferred_element_type=jnp.float32)
        total = part_sum if total is None else total + part_sum
        blended = part if blended is None else blended + part
    return blended / total, peak * (SCALE * LOG2E), total


def cols(chunk, width=BW, base=0):
    return pl.ds(pl.multiple_of(base + chunk * width, 128), width)


def head_cols(head, base=0):
    return pl.ds(pl.multiple_of(base + head * HDIM, 128), HDIM)


def self_kernel(with_prompts, *refs):
    if with_prompts:
        (q_hbm, kv_hbm, sink_hbm, prompt_hbm, cq_hbm, pick_ref, out_ref, cross_ref, *refs) = refs
        (bank, cq_ref, pr_s, pr_r, *refs) = refs
    else:
        (q_hbm, kv_hbm, sink_hbm, out_ref, *refs) = refs
    (q_ref, kv_ref, own_out, own_level, load_sem, kv_prev, sinks, q_in, o_send, o_recv, st_send, st_recv,
     kv_s, kv_r, q_s, q_r, s_s, s_r, o_s, o_r, st_s, st_r) = refs
    stride = lax.axis_size("span") // WIN
    me = lax.axis_index("span")
    place = me // stride
    stream = me % stride
    across = (stream + 2) % 4
    beside = stream + 1 - 2 * (stream % 2)
    rows_s = sink_hbm.shape[0]
    rows = q_ref.shape[0]
    mine = pl.ds(pl.multiple_of(place * rows_s, rows_s), rows_s)

    loads = {
        "sink": pltpu.make_async_copy(sink_hbm, sinks.at[mine, :], load_sem.at[0]),
        "q": pltpu.make_async_copy(q_hbm, q_ref, load_sem.at[1]),
        "kv": pltpu.make_async_copy(kv_hbm, kv_ref, load_sem.at[2]),
    }
    if with_prompts:
        loads["prompt"] = pltpu.make_async_copy(
            prompt_hbm, bank.at[place, stream], load_sem.at[3]
        )
        loads["cq"] = pltpu.make_async_copy(cq_hbm, cq_ref, load_sem.at[4])

    def load(*names):
        for name in names:
            if name in loads:
                loads[name].start()

    def loaded(*names):
        for name in names:
            if name in loads:
                loads[name].wait()

    def at_place(index):
        return {"span": index * stride + stream}

    def remote(src, dst, send, recv, index, line=None):
        return pltpu.make_async_remote_copy(
            src_ref=src, dst_ref=dst, send_sem=send, recv_sem=recv,
            device_id=at_place(index) if line is None else {"span": index * stride + line},
            device_id_type=MESH,
        )

    def kv_copies(chunk):
        pairs = []
        for part in range(2):
            where = cols(chunk, BW, part * WIDTH)
            pairs.append((sinks.at[0:rows_s, where], sinks.at[0:rows_s, where]))
        for part in range(2):
            where = cols(chunk, BW, part * WIDTH)
            pairs.append((kv_ref.at[:, where], kv_prev.at[:, where]))
        return [
            remote(src, dst, kv_s.at[i, chunk], kv_r.at[i, chunk], 1)
            for i, (src, dst) in enumerate(pairs)
        ]

    def q_copy(chunk, slot, index):
        return remote(
            q_ref.at[:, cols(chunk)], q_in.at[slot, :, cols(chunk)],
            q_s.at[slot, chunk], q_r.at[slot, chunk], index,
        )

    def q_relay(chunk):
        return remote(
            q_in.at[0, :, cols(chunk)], q_in.at[1, :, cols(chunk)],
            q_s.at[1, chunk], q_r.at[1, chunk], 1,
        )

    def sink_whole(which, index):
        where = sinks.at[which * rows_s : (which + 1) * rows_s, :]
        return remote(where, where, s_s.at[which, 0, 0], s_r.at[which, 0, 0], index)

    def sink_chunk(which, chunk, index):
        copies = []
        for part in range(2):
            where = cols(chunk, BW, part * WIDTH)
            piece = sinks.at[which * rows_s : (which + 1) * rows_s, where]
            copies.append(remote(
                piece, piece, s_s.at[which, chunk, part], s_r.at[which, chunk, part], index
            ))
        return copies

    def lift_copies(frame):
        lane = LAST * (1 - frame)
        copies = []
        for part in range(2):
            where = cols(LAST, BW, part * WIDTH)
            piece = sinks.at[frame * rows_s : (frame + 1) * rows_s, where]
            copies.append(remote(piece, piece, kv_s.at[part, lane], kv_r.at[part, lane], 2))
        for part in range(2):
            where = cols(LAST, BW, part * WIDTH)
            src = (kv_ref if frame else kv_prev).at[:, where]
            dst = kv_prev.at[:, cols(lane, BW, part * WIDTH)]
            copies.append(remote(src, dst, kv_s.at[2 + part, lane], kv_r.at[2 + part, lane], 2))
        return copies

    def o_copy(chunk, slot, index):
        return remote(
            o_send.at[slot, :, cols(chunk)], o_recv.at[slot, :, cols(chunk)],
            o_s.at[slot, chunk], o_r.at[slot, chunk], index,
        )

    def st_copy(chunk, slot, index):
        return remote(
            st_send.at[slot, chunk], st_recv.at[slot, chunk],
            st_s.at[slot, chunk], st_r.at[slot, chunk], index,
        )

    def partial(slot, chunk, pieces_of, index):
        lanes = lax.broadcasted_iota(jnp.int32, (rows, 128), 1)
        stats = jnp.zeros((rows, 128), jnp.float32)
        for inner in range(BUNDLE):
            head = chunk * BUNDLE + inner
            blended, peak, total = attend(q_in[slot, :, head_cols(head)], pieces_of(head))
            o_send[slot, :, head_cols(head)] = blended.astype(jnp.bfloat16)
            stats = jnp.where(lanes == inner, peak + jnp.log2(total), stats)
        st_send[slot, chunk] = jnp.transpose(stats)[0:8]
        o_copy(chunk, slot, index).start()
        st_copy(chunk, slot, index).start()

    def drain_partial(slot, index, chunks):
        def drain(chunk, carry):
            o_copy(chunk, slot, index).wait_send()
            st_copy(chunk, slot, index).wait_send()
            return carry
        lax.fori_loop(0, chunks, drain, 0)

    def own_part(chunk, pieces_of):
        lanes = lax.broadcasted_iota(jnp.int32, (rows, 128), 1)
        stats = jnp.zeros((rows, 128), jnp.float32)
        for inner in range(BUNDLE):
            head = chunk * BUNDLE + inner
            blended, peak, total = attend(q_ref[:, head_cols(head)], pieces_of(head))
            own_out[:, head_cols(head)] = blended
            stats = jnp.where(lanes == inner, peak + jnp.log2(total), stats)
        own_level[chunk] = stats

    def final(chunk, pieces_of, slots, index, own=True):
        levels_in = [own_level[chunk]] if own else []
        for slot in slots:
            o_copy(chunk, slot, index).wait_recv()
            st_copy(chunk, slot, index).wait_recv()
            padded = jnp.concatenate(
                [st_recv[slot, chunk], jnp.zeros((120, rows), jnp.float32)], axis=0
            )
            levels_in.append(jnp.transpose(padded))
        for inner in range(BUNDLE):
            head = chunk * BUNDLE + inner
            where = head_cols(head)
            outs = [own_out[:, where]] if own else []
            outs += [o_recv[slot, :, where].astype(jnp.float32) for slot in slots]
            levels = [level[:, inner : inner + 1] for level in levels_in]
            if pieces_of is not None:
                blended, peak, total = attend(q_ref[:, where], pieces_of(head))
                outs.append(blended)
                levels.append(peak + jnp.log2(total))
            if len(outs) > 1:
                top = functools.reduce(jnp.maximum, levels)
                shares = [jnp.exp2(level - top) for level in levels]
                whole = functools.reduce(jnp.add, shares)
                blended = functools.reduce(
                    jnp.add, [out * share for out, share in zip(outs, shares)]
                ) / whole
            else:
                blended = outs[0]
            out_ref[:, where] = blended.astype(jnp.bfloat16)

    def loop(low, high, body):
        def step(chunk, carry):
            body(chunk)
            return carry
        lax.fori_loop(low, high, step, 0)

    def turn(step):
        return jnp.where(step < 2, step + 2, jnp.where(step < LAST, step - 2, LAST))

    def pair(ref, head, low=None, high=None):
        part = slice(low, high)
        return ref[part, head_cols(head)], ref[part, head_cols(head, WIDTH)]

    def prompt_copy(kind, piece, line, index, to_line):
        return remote(
            bank.at[piece, line], bank.at[piece, line],
            pr_s.at[kind, piece], pr_r.at[kind if kind > 1 else 0, piece], index, to_line,
        )

    def line_copies(here, piece, kinds=(0, 1, 2, 3)):
        copies = []
        if 0 in kinds and piece <= here < WIN - 1:
            copies.append(prompt_copy(0, piece, stream, here + 1, stream))
        if 1 in kinds and 0 < here <= piece:
            copies.append(prompt_copy(1, piece, stream, here - 1, stream))
        if 2 in kinds:
            copies.append(prompt_copy(2, piece, stream, here, across))
        if 3 in kinds:
            copies.append(prompt_copy(3, piece, stream, here, beside))
        return copies

    def spread(here, piece, kinds=(0, 1, 2, 3)):
        if not with_prompts:
            return
        if piece != here:
            prompt_copy(0, piece, stream, here, stream).wait_recv()
        for copy in line_copies(here, piece, kinds):
            copy.start()

    def spread_across(here, pieces):
        if not with_prompts:
            return
        for piece in pieces:
            prompt_copy(2, piece, across, here, stream).wait_recv()
            prompt_copy(4, piece, across, here, beside).start()

    def cross(here):
        if not with_prompts:
            return
        loaded("cq")
        for piece in range(WIN):
            prompt_copy(3, piece, beside, here, stream).wait_recv()
            prompt_copy(4, piece, 3 - stream, here, stream).wait_recv()
        pick = (place >= pick_ref[stream]).astype(jnp.int32)
        tokens = bank.shape[0] * bank.shape[1] * bank.shape[3]

        def chunk_of(chunk):
            for inner in range(BUNDLE):
                head = chunk * BUNDLE + inner
                keys = bank[:, :, pick, :, head_cols(head)].reshape(tokens, HDIM)
                values = bank[:, :, pick, :, head_cols(head, WIDTH)].reshape(tokens, HDIM)
                blended, _, _ = attend(cq_ref[:, head_cols(head)], [(keys, values)])
                cross_ref[:, head_cols(head)] = blended.astype(jnp.bfloat16)
        loop(0, CHUNKS, chunk_of)

    def drain_prompts(here):
        if not with_prompts:
            return
        for piece in range(WIN):
            for copy in line_copies(here, piece):
                copy.wait_send()
            prompt_copy(4, piece, across, here, beside).wait_send()

    barrier = pltpu.get_barrier_semaphore()
    greeted = [at_place((place + step) % WIN) for step in range(1, WIN)]
    if with_prompts:
        greeted += [{"span": place * stride + across}, {"span": place * stride + beside}]
    for other in greeted:
        pl.semaphore_signal(barrier, inc=1, device_id=other, device_id_type=MESH)
    load("q", "prompt", "sink", "kv", "cq")
    pl.semaphore_wait(barrier, len(greeted))

    @pl.when(place == 0)
    def _():
        loaded("prompt")
        spread(0, 0)
        loaded("sink", "kv")

        def send(chunk):
            for copy in kv_copies(chunk):
                copy.start()
        loop(0, 2, send)
        send(LAST)
        loop(2, LAST, send)
        spread(0, 1)
        spread_across(0, (0, 1))
        loaded("q")
        sink_whole(1, 0).wait_recv()
        loop(0, CHUNKS, lambda chunk: own_part(
            chunk, lambda head: [pair(sinks, head, 0, 2 * rows_s), pair(kv_ref, head)]
        ))
        spread(0, 2)
        spread_across(0, (2,))
        spread(0, 3)
        spread_across(0, (3,))
        cross(0)

        def ending(step):
            chunk = turn(step)
            for which in (2, 3):
                for copy in sink_chunk(which, chunk, 0):
                    copy.wait_recv()
            final(chunk, lambda head: [pair(sinks, head, 2 * rows_s, 4 * rows_s)], (), 0)
        loop(0, CHUNKS, ending)

        def drain(chunk):
            for copy in kv_copies(chunk):
                copy.wait_send()
        loop(0, CHUNKS, drain)
        drain_prompts(0)

    @pl.when(place == 1)
    def _():
        loaded("prompt")
        spread(1, 1)
        loaded("sink", "kv")
        for copy in lift_copies(1):
            copy.start()
        sink_whole(1, 0).start()

        def work(chunk):
            for copy in kv_copies(chunk):
                copy.wait_recv()

            def both(slot):
                q_copy(chunk, slot, 1).wait_recv()
                partial(
                    slot, chunk,
                    lambda head: [
                        pair(sinks, head, 0, 2 * rows_s), pair(kv_prev, head), pair(kv_ref, head)
                    ],
                    2 + slot,
                )
            loop(0, 2, both)

        def own(chunk):
            own_part(chunk, lambda head: [
                pair(sinks, head, 0, 2 * rows_s), pair(kv_prev, head), pair(kv_ref, head)
            ])

        def pass_sink(which, chunk):
            for copy in sink_chunk(which, chunk, 1):
                copy.wait_recv()
            for copy in sink_chunk(which, chunk, 0):
                copy.start()

        def lift():
            for copy in kv_copies(LAST):
                copy.wait_recv()
            for copy in lift_copies(0):
                copy.start()

        spread(1, 0)
        spread_across(1, (1, 0))
        loaded("q")

        def early(step):
            chunk = jnp.where(step == 2, LAST, jnp.where(step > 2, step - 1, step))

            @pl.when(step != 2)
            def _():
                work(chunk)

            @pl.when(step == 3)
            def _():
                spread_across(1, (3,))
                loop(3, CHUNKS, lambda piece: pass_sink(2, turn(piece)))
                cross(1)

            @pl.when(step < 3)
            def _():
                own(chunk)

            @pl.when(step == 0)
            def _():
                spread(1, 2)
                spread_across(1, (2,))

            @pl.when(step == 1)
            def _():
                spread(1, 3)
                lift()

            @pl.when(step == 2)
            def _():
                loop(0, 3, lambda piece: pass_sink(2, turn(piece)))
        loop(0, CHUNKS, early)

        def ending(step):
            chunk = turn(step)
            pass_sink(3, chunk)

            @pl.when(step < 2)
            def _():
                final(chunk, lambda head: [
                    pair(sinks, head), pair(kv_prev, head), pair(kv_ref, head)
                ], (), 1, False)

            @pl.when(step >= 2)
            def _():
                final(chunk, lambda head: [pair(sinks, head, 2 * rows_s, 4 * rows_s)], (), 1)
        loop(0, CHUNKS, ending)
        sink_whole(1, 0).wait_send()

        def drain(chunk):
            for which in (2, 3):
                for copy in sink_chunk(which, chunk, 0):
                    copy.wait_send()
        loop(0, CHUNKS, drain)
        for frame in range(2):
            for copy in lift_copies(frame):
                copy.wait_send()
        for slot in range(2):
            drain_partial(slot, 2 + slot, LAST)
        drain_prompts(1)

    @pl.when(place == 2)
    def _():
        def send(chunk):
            q_copy(chunk, 0, 1).start()

        def relay(chunk):
            q_copy(chunk, 0, 2).wait_recv()
            q_relay(chunk).start()

        def work(chunk):
            partial(
                0, chunk,
                lambda head: [pair(sinks, head, 2 * rows_s, 3 * rows_s), pair(kv_ref, head)], 3,
            )

        def send_sink(which):
            def body(step):
                for copy in sink_chunk(which, turn(step), 1):
                    copy.start()
            loop(0, CHUNKS, body)

        loaded("q")
        loop(0, 2, send)
        loaded("prompt")
        spread(2, 2, (0, 2, 3))
        loop(0, 2, relay)
        spread(2, 2, (1,))
        loaded("sink", "kv")
        loop(0, 2, work)
        spread(2, 1)
        spread_across(2, (2, 1))
        spread(2, 3)

        def forward(chunk):
            send(chunk)
            relay(chunk)
        loop(2, 3, forward)
        send_sink(2)
        loop(3, LAST, forward)
        loop(2, LAST, work)
        spread_across(2, (3,))
        spread(2, 0)
        sink_whole(3, 2).wait_recv()
        send_sink(3)
        spread_across(2, (0,))
        loop(0, LAST, lambda chunk: own_part(
            chunk, lambda head: [pair(sinks, head, 2 * rows_s, 4 * rows_s), pair(kv_ref, head)]
        ))
        cross(2)

        def ending(chunk):
            final(chunk, None, (0,), 2)
        loop(0, 2, ending)
        for frame in (1, 0):
            for copy in lift_copies(frame):
                copy.wait_recv()
        q_copy(LAST, 0, 2).wait_recv()

        def lifted(head, high):
            return [
                pair(sinks, head, 0, high), pair(kv_prev, head),
                pair(kv_prev, head - LAST * BUNDLE), pair(kv_ref, head),
            ]
        partial(0, LAST, lambda head: lifted(head, 3 * rows_s), 3)
        final(LAST, lambda head: lifted(head, 4 * rows_s), (), 2, False)
        loop(2, LAST, ending)

        def drain(chunk):
            for which in (2, 3):
                for copy in sink_chunk(which, chunk, 1):
                    copy.wait_send()
        loop(0, CHUNKS, drain)
        loop(0, LAST, lambda chunk: q_copy(chunk, 0, 1).wait_send())
        loop(0, LAST, lambda chunk: q_relay(chunk).wait_send())
        drain_partial(0, 3, CHUNKS)
        drain_prompts(2)

    @pl.when(place == 3)
    def _():
        loaded("q")
        loop(0, 2, lambda chunk: q_copy(chunk, 0, 2).start())
        loaded("prompt")
        spread(3, 3)
        loop(2, CHUNKS, lambda chunk: q_copy(chunk, 0, 2).start())
        loaded("sink")
        sink_whole(3, 2).start()
        loaded("kv")
        loop(0, CHUNKS, lambda chunk: own_part(
            chunk,
            lambda head: [pair(sinks, head, 3 * rows_s, 4 * rows_s), pair(kv_ref, head)],
        ))
        spread(3, 2)
        spread_across(3, (3, 2))
        spread(3, 1)
        spread_across(3, (1,))
        spread(3, 0)
        spread_across(3, (0,))
        cross(3)

        def ending(chunk, slots=(0, 1)):
            final(chunk, None, slots, 3)
        loop(0, 2, ending)
        ending(LAST, (0,))
        loop(2, LAST, ending)
        sink_whole(3, 2).wait_send()
        loop(0, CHUNKS, lambda chunk: q_copy(chunk, 0, 2).wait_send())
        drain_prompts(3)


def store_kernel(*refs):
    half = len(refs) // 2
    sems = refs[-1]
    copies = []
    for i in range(half):
        rows = refs[i].shape[0] // STORES
        for j in range(STORES):
            part = slice(j * rows, (j + 1) * rows)
            copies.append(pltpu.make_async_copy(
                refs[i].at[part, :], refs[half + i].at[part, :], sems.at[i, j]
            ))
    for copy in copies:
        copy.start()
    for copy in copies:
        copy.wait()


def self_attention(queries, frame_kv, own_sink, prompts=None):
    rows = queries.shape[0]
    vmem = pl.BlockSpec(memory_space=pltpu.VMEM)
    hbm = pl.BlockSpec(memory_space=pltpu.HBM)
    dma = pltpu.SemaphoreType.DMA
    operands = [queries, frame_kv, own_sink]
    in_specs = [hbm] * 3
    outs = [jax.ShapeDtypeStruct((rows, WIDTH), jnp.bfloat16)]
    scratch = []
    if prompts is not None:
        operands += prompts
        in_specs += [hbm, hbm, pl.BlockSpec(memory_space=pltpu.SMEM)]
        outs = outs * 2
        scratch = [
            pltpu.VMEM((WIN, lax.axis_size("span") // WIN) + prompts[0].shape, jnp.bfloat16),
            pltpu.VMEM((rows, WIDTH), jnp.bfloat16),
            dma((5, WIN)), dma((5, WIN)),
        ]
    results = pl.pallas_call(
        functools.partial(self_kernel, prompts is not None),
        out_shape=[pltpu.VMEM(out.shape, out.dtype) for out in outs],
        in_specs=in_specs,
        out_specs=[vmem] * len(outs),
        scratch_shapes=scratch + [
            pltpu.VMEM((rows, WIDTH), jnp.bfloat16),
            pltpu.VMEM((rows, 2 * WIDTH), jnp.bfloat16),
            pltpu.VMEM((rows, WIDTH), jnp.float32),
            pltpu.VMEM((CHUNKS, rows, 128), jnp.float32),
            dma((5,)),
            pltpu.VMEM((rows, 2 * WIDTH), jnp.bfloat16),
            pltpu.VMEM((WIN * own_sink.shape[0], 2 * WIDTH), jnp.bfloat16),
            pltpu.VMEM((2, rows, WIDTH), jnp.bfloat16),
            pltpu.VMEM((2, rows, WIDTH), jnp.bfloat16),
            pltpu.VMEM((2, rows, WIDTH), jnp.bfloat16),
            pltpu.VMEM((2, CHUNKS, 8, rows), jnp.float32),
            pltpu.VMEM((2, CHUNKS, 8, rows), jnp.float32),
            dma((4, CHUNKS)), dma((4, CHUNKS)),
            dma((2, CHUNKS)), dma((2, CHUNKS)),
            dma((WIN, CHUNKS, 2)), dma((WIN, CHUNKS, 2)),
            dma((2, CHUNKS)), dma((2, CHUNKS)),
            dma((2, CHUNKS)), dma((2, CHUNKS)),
        ],
        compiler_params=pltpu.CompilerParams(
            collective_id=0, has_side_effects=True, vmem_limit_bytes=48 * 1024 * 1024
        ),
    )(*[pltpu.with_memory_space_constraint(x, pltpu.HBM) for x in operands])
    return pl.pallas_call(
        store_kernel,
        out_shape=outs,
        in_specs=[pl.BlockSpec(memory_space=pl.ANY)] * len(outs),
        out_specs=[pl.BlockSpec(memory_space=pl.ANY)] * len(outs),
        scratch_shapes=[dma((len(outs), STORES))],
    )(*[pltpu.with_memory_space_constraint(x, pltpu.VMEM) for x in results])


def cross_kernel(pick_ref, q_ref, k_ref, v_ref, out_ref):
    for inner in range(BUNDLE):
        where = slice(inner * HDIM, (inner + 1) * HDIM)
        blended, _, _ = attend(q_ref[:, where], [(k_ref[0, :, where], v_ref[0, :, where])])
        out_ref[:, where] = blended.astype(jnp.bfloat16)


def cross_attention(cross_queries, prompts, pick):
    rows = cross_queries.shape[0]
    tokens = prompts.shape[1]
    return pl.pallas_call(
        cross_kernel,
        out_shape=jax.ShapeDtypeStruct((rows, WIDTH), jnp.bfloat16),
        grid_spec=pltpu.PrefetchScalarGridSpec(
            num_scalar_prefetch=1,
            grid=(CHUNKS,),
            in_specs=[
                pl.BlockSpec((rows, BW), lambda c, pick: (0, c)),
                pl.BlockSpec((1, tokens, BW), lambda c, pick: (pick[0], 0, c)),
                pl.BlockSpec((1, tokens, BW), lambda c, pick: (pick[0], 0, CHUNKS + c)),
            ],
            out_specs=pl.BlockSpec((rows, BW), lambda c, pick: (0, c)),
        ),
    )(pick.reshape(1), cross_queries, prompts, prompts)


def shards(queries, cross_queries, frame_kv, sink_kv, prompt_kv, switch):
    stream_count = lax.axis_size("span") // WIN
    device = lax.axis_index("span")
    place = device // stream_count
    stream_of = device % stream_count
    own_sink = sink_kv.reshape(sink_kv.shape[1], sink_kv.shape[2])
    if stream_count == 4 and prompt_kv.shape[1] % 16 == 0:
        return tuple(
            self_attention(queries, frame_kv, own_sink, [prompt_kv, cross_queries, switch])
        )
    stream_ids = jnp.arange(switch.shape[0], dtype=jnp.int32)
    switch_at = jnp.sum(jnp.where(stream_ids == stream_of, switch, 0))
    pick = (place >= switch_at).astype(jnp.int32)
    prompts = lax.all_gather(prompt_kv, "span", axis=1, tiled=True)
    (self_out,) = self_attention(queries, frame_kv, own_sink)
    cross_out = cross_attention(cross_queries, prompts, pick)
    return (self_out, cross_out)


def solution(mesh):
    in_specs = (
        P(("groups", "span"), None),
        P(("groups", "span"), None),
        P(("groups", "span"), None),
        P(("groups", "span"), None, None),
        P("groups", "span", None),
        P("groups"),
    )
    out_specs = (P(("groups", "span"), None), P(("groups", "span"), None))
    return jax.shard_map(shards, mesh=mesh, in_specs=in_specs, out_specs=out_specs, check_vma=False)
```

```python
import functools
import math

import jax
import jax.numpy as jnp
from jax import lax
from jax.experimental import pallas as pl
from jax.experimental.pallas import tpu as pltpu
from jax.sharding import PartitionSpec as P

HEADS = 20
HDIM = 128
WIN = 4
BUNDLE = 5
CHUNKS = HEADS // BUNDLE
LAST = CHUNKS - 1
STORES = 1
BW = BUNDLE * HDIM
WIDTH = HEADS * HDIM
SCALE = 1.0 / math.sqrt(HDIM)
LOG2E = 1.4426950408889634
MESH = pl.DeviceIdType.MESH


def attend(query, pieces):
    scores = [
        lax.dot_general(query, keys, (((1,), (1,)), ((), ())), preferred_element_type=jnp.float32)
        for keys, _ in pieces
    ]
    peak = functools.reduce(
        jnp.maximum, [jnp.max(piece, axis=1, keepdims=True) for piece in scores]
    )
    total, blended = None, None
    for piece, (_, values) in zip(scores, pieces):
        weights = jnp.exp2((piece - peak) * (SCALE * LOG2E))
        part_sum = jnp.sum(weights, axis=1, keepdims=True)
        part = jnp.dot(weights.astype(jnp.bfloat16), values, preferred_element_type=jnp.float32)
        total = part_sum if total is None else total + part_sum
        blended = part if blended is None else blended + part
    return blended / total, peak * (SCALE * LOG2E), total


def cols(chunk, width=BW, base=0):
    return pl.ds(pl.multiple_of(base + chunk * width, 128), width)


def head_cols(head, base=0):
    return pl.ds(pl.multiple_of(base + head * HDIM, 128), HDIM)


def self_kernel(with_prompts, *refs):
    if with_prompts:
        (q_hbm, kv_hbm, sink_hbm, prompt_hbm, cq_hbm, pick_ref, out_ref, cross_ref, *refs) = refs
        (bank, cq_ref, pr_s, pr_r, *refs) = refs
    else:
        (q_hbm, kv_hbm, sink_hbm, out_ref, *refs) = refs
    (q_ref, kv_ref, own_out, own_level, load_sem, kv_prev, sinks, q_in, o_send, o_recv, st_send, st_recv,
     kv_s, kv_r, q_s, q_r, s_s, s_r, o_s, o_r, st_s, st_r) = refs
    stride = lax.axis_size("span") // WIN
    me = lax.axis_index("span")
    place = me // stride
    stream = me % stride
    across = (stream + 2) % 4
    beside = stream + 1 - 2 * (stream % 2)
    rows_s = sink_hbm.shape[0]
    rows = q_ref.shape[0]
    mine = pl.ds(pl.multiple_of(place * rows_s, rows_s), rows_s)

    loads = {
        "sink": pltpu.make_async_copy(sink_hbm, sinks.at[mine, :], load_sem.at[0]),
        "q": pltpu.make_async_copy(q_hbm, q_ref, load_sem.at[1]),
        "kv": pltpu.make_async_copy(kv_hbm, kv_ref, load_sem.at[2]),
    }
    if with_prompts:
        loads["prompt"] = pltpu.make_async_copy(
            prompt_hbm, bank.at[place, stream], load_sem.at[3]
        )
        loads["cq"] = pltpu.make_async_copy(cq_hbm, cq_ref, load_sem.at[4])

    def load(*names):
        for name in names:
            if name in loads:
                loads[name].start()

    def loaded(*names):
        for name in names:
            if name in loads:
                loads[name].wait()

    def at_place(index):
        return {"span": index * stride + stream}

    def remote(src, dst, send, recv, index, line=None):
        return pltpu.make_async_remote_copy(
            src_ref=src, dst_ref=dst, send_sem=send, recv_sem=recv,
            device_id=at_place(index) if line is None else {"span": index * stride + line},
            device_id_type=MESH,
        )

    def kv_copies(chunk):
        pairs = []
        for part in range(2):
            where = cols(chunk, BW, part * WIDTH)
            pairs.append((sinks.at[0:rows_s, where], sinks.at[0:rows_s, where]))
        for part in range(2):
            where = cols(chunk, BW, part * WIDTH)
            pairs.append((kv_ref.at[:, where], kv_prev.at[:, where]))
        return [
            remote(src, dst, kv_s.at[i, chunk], kv_r.at[i, chunk], 1)
            for i, (src, dst) in enumerate(pairs)
        ]

    def q_copy(chunk, slot, index):
        return remote(
            q_ref.at[:, cols(chunk)], q_in.at[slot, :, cols(chunk)],
            q_s.at[slot, chunk], q_r.at[slot, chunk], index,
        )

    def q_relay(chunk):
        return remote(
            q_in.at[0, :, cols(chunk)], q_in.at[1, :, cols(chunk)],
            q_s.at[1, chunk], q_r.at[1, chunk], 1,
        )

    def sink_whole(which, index):
        where = sinks.at[which * rows_s : (which + 1) * rows_s, :]
        return remote(where, where, s_s.at[which, 0, 0], s_r.at[which, 0, 0], index)

    def sink_chunk(which, chunk, index):
        copies = []
        for part in range(2):
            where = cols(chunk, BW, part * WIDTH)
            piece = sinks.at[which * rows_s : (which + 1) * rows_s, where]
            copies.append(remote(
                piece, piece, s_s.at[which, chunk, part], s_r.at[which, chunk, part], index
            ))
        return copies

    def lift_copies(frame):
        lane = LAST * (1 - frame)
        copies = []
        for part in range(2):
            where = cols(LAST, BW, part * WIDTH)
            piece = sinks.at[frame * rows_s : (frame + 1) * rows_s, where]
            copies.append(remote(piece, piece, kv_s.at[part, lane], kv_r.at[part, lane], 2))
        for part in range(2):
            where = cols(LAST, BW, part * WIDTH)
            src = (kv_ref if frame else kv_prev).at[:, where]
            dst = kv_prev.at[:, cols(lane, BW, part * WIDTH)]
            copies.append(remote(src, dst, kv_s.at[2 + part, lane], kv_r.at[2 + part, lane], 2))
        return copies

    def o_copy(chunk, slot, index):
        return remote(
            o_send.at[slot, :, cols(chunk)], o_recv.at[slot, :, cols(chunk)],
            o_s.at[slot, chunk], o_r.at[slot, chunk], index,
        )

    def st_copy(chunk, slot, index):
        return remote(
            st_send.at[slot, chunk], st_recv.at[slot, chunk],
            st_s.at[slot, chunk], st_r.at[slot, chunk], index,
        )

    def partial(slot, chunk, pieces_of, index):
        lanes = lax.broadcasted_iota(jnp.int32, (rows, 128), 1)
        stats = jnp.zeros((rows, 128), jnp.float32)
        for inner in range(BUNDLE):
            head = chunk * BUNDLE + inner
            blended, peak, total = attend(q_in[slot, :, head_cols(head)], pieces_of(head))
            o_send[slot, :, head_cols(head)] = blended.astype(jnp.bfloat16)
            stats = jnp.where(lanes == inner, peak + jnp.log2(total), stats)
        st_send[slot, chunk] = jnp.transpose(stats)[0:8]
        o_copy(chunk, slot, index).start()
        st_copy(chunk, slot, index).start()

    def drain_partial(slot, index, chunks):
        def drain(chunk, carry):
            o_copy(chunk, slot, index).wait_send()
            st_copy(chunk, slot, index).wait_send()
            return carry
        lax.fori_loop(0, chunks, drain, 0)

    def own_part(chunk, pieces_of):
        lanes = lax.broadcasted_iota(jnp.int32, (rows, 128), 1)
        stats = jnp.zeros((rows, 128), jnp.float32)
        for inner in range(BUNDLE):
            head = chunk * BUNDLE + inner
            blended, peak, total = attend(q_ref[:, head_cols(head)], pieces_of(head))
            own_out[:, head_cols(head)] = blended
            stats = jnp.where(lanes == inner, peak + jnp.log2(total), stats)
        own_level[chunk] = stats

    def final(chunk, pieces_of, slots, index, own=True):
        levels_in = [own_level[chunk]] if own else []
        for slot in slots:
            o_copy(chunk, slot, index).wait_recv()
            st_copy(chunk, slot, index).wait_recv()
            padded = jnp.concatenate(
                [st_recv[slot, chunk], jnp.zeros((120, rows), jnp.float32)], axis=0
            )
            levels_in.append(jnp.transpose(padded))
        for inner in range(BUNDLE):
            head = chunk * BUNDLE + inner
            where = head_cols(head)
            outs = [own_out[:, where]] if own else []
            outs += [o_recv[slot, :, where].astype(jnp.float32) for slot in slots]
            levels = [level[:, inner : inner + 1] for level in levels_in]
            if pieces_of is not None:
                blended, peak, total = attend(q_ref[:, where], pieces_of(head))
                outs.append(blended)
                levels.append(peak + jnp.log2(total))
            if len(outs) > 1:
                top = functools.reduce(jnp.maximum, levels)
                shares = [jnp.exp2(level - top) for level in levels]
                whole = functools.reduce(jnp.add, shares)
                blended = functools.reduce(
                    jnp.add, [out * share for out, share in zip(outs, shares)]
                ) / whole
            else:
                blended = outs[0]
            out_ref[:, where] = blended.astype(jnp.bfloat16)

    def loop(low, high, body):
        def step(chunk, carry):
            body(chunk)
            return carry
        lax.fori_loop(low, high, step, 0)

    def turn(step):
        return jnp.where(step < 2, step + 1, jnp.where(step < LAST, 0, LAST))

    def pair(ref, head, low=None, high=None):
        part = slice(low, high)
        return ref[part, head_cols(head)], ref[part, head_cols(head, WIDTH)]

    def prompt_copy(kind, piece, line, index, to_line):
        return remote(
            bank.at[piece, line], bank.at[piece, line],
            pr_s.at[kind, piece], pr_r.at[kind if kind > 1 else 0, piece], index, to_line,
        )

    def line_copies(here, piece, kinds=(0, 1, 2, 3)):
        copies = []
        if 0 in kinds and piece <= here < WIN - 1:
            copies.append(prompt_copy(0, piece, stream, here + 1, stream))
        if 1 in kinds and 0 < here <= piece:
            copies.append(prompt_copy(1, piece, stream, here - 1, stream))
        if 2 in kinds:
            copies.append(prompt_copy(2, piece, stream, here, across))
        if 3 in kinds:
            copies.append(prompt_copy(3, piece, stream, here, beside))
        return copies

    def spread(here, piece, kinds=(0, 1, 2, 3)):
        if not with_prompts:
            return
        if piece != here:
            prompt_copy(0, piece, stream, here, stream).wait_recv()
        for copy in line_copies(here, piece, kinds):
            copy.start()

    def spread_across(here, pieces):
        if not with_prompts:
            return
        for piece in pieces:
            prompt_copy(2, piece, across, here, stream).wait_recv()
            prompt_copy(4, piece, across, here, beside).start()

    def cross(here):
        if not with_prompts:
            return
        loaded("cq")
        for piece in range(WIN):
            prompt_copy(3, piece, beside, here, stream).wait_recv()
            prompt_copy(4, piece, 3 - stream, here, stream).wait_recv()
        pick = (place >= pick_ref[stream]).astype(jnp.int32)
        tokens = bank.shape[0] * bank.shape[1] * bank.shape[3]

        def chunk_of(chunk):
            for inner in range(BUNDLE):
                head = chunk * BUNDLE + inner
                keys = bank[:, :, pick, :, head_cols(head)].reshape(tokens, HDIM)
                values = bank[:, :, pick, :, head_cols(head, WIDTH)].reshape(tokens, HDIM)
                blended, _, _ = attend(cq_ref[:, head_cols(head)], [(keys, values)])
                cross_ref[:, head_cols(head)] = blended.astype(jnp.bfloat16)
        loop(0, CHUNKS, chunk_of)

    def drain_prompts(here):
        if not with_prompts:
            return
        for piece in range(WIN):
            for copy in line_copies(here, piece):
                copy.wait_send()
            prompt_copy(4, piece, across, here, beside).wait_send()

    barrier = pltpu.get_barrier_semaphore()
    load("q", "prompt", "sink", "kv", "cq")
    for here, others in enumerate(((1,), (0, 2, 3), (1, 3), (1, 2))):
        @pl.when(place == here)
        def _(others=others):
            for other in others:
                pl.semaphore_signal(
                    barrier, inc=1, device_id=at_place(other), device_id_type=MESH
                )
    if with_prompts:
        for line in (across, beside):
            pl.semaphore_signal(
                barrier, inc=1, device_id={"span": place * stride + line}, device_id_type=MESH
            )

    def greeted(count):
        pl.semaphore_wait(barrier, count + (2 if with_prompts else 0))

    @pl.when(place == 0)
    def _():
        greeted(1)
        loaded("prompt")
        spread(0, 0)
        loaded("sink", "kv")

        def send(chunk):
            for copy in kv_copies(chunk):
                copy.start()
        send(0)
        send(LAST)
        loop(1, LAST, send)
        spread(0, 1)
        spread_across(0, (0, 1))
        loaded("q")
        sink_whole(1, 0).wait_recv()
        loop(0, CHUNKS, lambda chunk: own_part(
            chunk, lambda head: [pair(sinks, head, 0, 2 * rows_s), pair(kv_ref, head)]
        ))
        spread(0, 2)
        spread_across(0, (2,))
        spread(0, 3)
        spread_across(0, (3,))
        cross(0)

        def ending(step):
            chunk = turn(step)
            for which in (2, 3):
                for copy in sink_chunk(which, chunk, 0):
                    copy.wait_recv()
            final(chunk, lambda head: [pair(sinks, head, 2 * rows_s, 4 * rows_s)], (), 0)
        loop(0, CHUNKS, ending)

        def drain(chunk):
            for copy in kv_copies(chunk):
                copy.wait_send()
        loop(0, CHUNKS, drain)
        drain_prompts(0)

    @pl.when(place == 1)
    def _():
        greeted(3)
        loaded("prompt")
        spread(1, 1)
        loaded("sink", "kv")
        for copy in lift_copies(1):
            copy.start()
        sink_whole(1, 0).start()

        def work(chunk):
            for copy in kv_copies(chunk):
                copy.wait_recv()

            def both(slot):
                q_copy(chunk, slot, 1).wait_recv()
                partial(
                    slot, chunk,
                    lambda head: [
                        pair(sinks, head, 0, 2 * rows_s), pair(kv_prev, head), pair(kv_ref, head)
                    ],
                    2 + slot,
                )
            loop(0, 2, both)

        def own(chunk):
            own_part(chunk, lambda head: [
                pair(sinks, head, 0, 2 * rows_s), pair(kv_prev, head), pair(kv_ref, head)
            ])

        def pass_sink(which, chunk):
            for copy in sink_chunk(which, chunk, 1):
                copy.wait_recv()
            for copy in sink_chunk(which, chunk, 0):
                copy.start()

        def lift():
            for copy in kv_copies(LAST):
                copy.wait_recv()
            for copy in lift_copies(0):
                copy.start()

        spread(1, 0)
        spread_across(1, (1, 0))
        loaded("q")

        def early(step):
            chunk = jnp.where(step == 1, LAST, jnp.where(step > 1, step - 1, step))

            @pl.when(step != 1)
            def _():
                work(chunk)

            @pl.when(step == 1)
            def _():
                spread(1, 3)
                lift()

            @pl.when(step == 2)
            def _():
                spread_across(1, (3,))
                loop(2, CHUNKS, lambda piece: pass_sink(2, turn(piece)))
                cross(1)

            @pl.when(step < 2)
            def _():
                own(chunk)

            @pl.when(step == 0)
            def _():
                spread(1, 2)
                spread_across(1, (2,))

            @pl.when(step == 1)
            def _():
                loop(0, 2, lambda piece: pass_sink(2, turn(piece)))
        loop(0, CHUNKS, early)

        def ending(step):
            chunk = turn(step)
            pass_sink(3, chunk)

            @pl.when(step < 2)
            def _():
                final(chunk, lambda head: [
                    pair(sinks, head), pair(kv_prev, head), pair(kv_ref, head)
                ], (), 1, False)

            @pl.when(step >= 2)
            def _():
                final(chunk, lambda head: [pair(sinks, head, 2 * rows_s, 4 * rows_s)], (), 1)
        loop(0, CHUNKS, ending)
        sink_whole(1, 0).wait_send()

        def drain(chunk):
            for which in (2, 3):
                for copy in sink_chunk(which, chunk, 0):
                    copy.wait_send()
        loop(0, CHUNKS, drain)
        for frame in range(2):
            for copy in lift_copies(frame):
                copy.wait_send()
        for slot in range(2):
            drain_partial(slot, 2 + slot, LAST)
        drain_prompts(1)

    @pl.when(place == 2)
    def _():
        greeted(2)

        def send(chunk):
            q_copy(chunk, 0, 1).start()

        def relay(chunk):
            q_copy(chunk, 0, 2).wait_recv()
            q_relay(chunk).start()

        def work(chunk):
            partial(
                0, chunk,
                lambda head: [pair(sinks, head, 2 * rows_s, 3 * rows_s), pair(kv_ref, head)], 3,
            )

        def send_sink(which):
            def body(step):
                for copy in sink_chunk(which, turn(step), 1):
                    copy.start()
            loop(0, CHUNKS, body)

        loaded("q")
        send(0)
        loaded("prompt")
        spread(2, 2, (0, 2, 3))
        relay(0)
        spread(2, 2, (1,))
        loaded("sink", "kv")
        work(0)
        spread(2, 1)
        spread_across(2, (2, 1))
        spread(2, 3)

        def forward(chunk):
            send(chunk)
            relay(chunk)
        forward(1)
        send_sink(2)
        loop(2, LAST, forward)
        loop(1, LAST, work)
        spread_across(2, (3,))
        spread(2, 0)
        sink_whole(3, 2).wait_recv()
        send_sink(3)
        spread_across(2, (0,))
        loop(0, LAST, lambda chunk: own_part(
            chunk, lambda head: [pair(sinks, head, 2 * rows_s, 4 * rows_s), pair(kv_ref, head)]
        ))
        cross(2)

        def ending(chunk):
            final(chunk, None, (0,), 2)
        ending(0)
        for frame in (1, 0):
            for copy in lift_copies(frame):
                copy.wait_recv()
        q_copy(LAST, 0, 2).wait_recv()

        def lifted(head, high):
            return [
                pair(sinks, head, 0, high), pair(kv_prev, head),
                pair(kv_prev, head - LAST * BUNDLE), pair(kv_ref, head),
            ]
        partial(0, LAST, lambda head: lifted(head, 3 * rows_s), 3)
        final(LAST, lambda head: lifted(head, 4 * rows_s), (), 2, False)
        loop(1, LAST, ending)

        def drain(chunk):
            for which in (2, 3):
                for copy in sink_chunk(which, chunk, 1):
                    copy.wait_send()
        loop(0, CHUNKS, drain)
        loop(0, LAST, lambda chunk: q_copy(chunk, 0, 1).wait_send())
        loop(0, LAST, lambda chunk: q_relay(chunk).wait_send())
        drain_partial(0, 3, CHUNKS)
        drain_prompts(2)

    @pl.when(place == 3)
    def _():
        greeted(2)
        loaded("q")
        q_copy(0, 0, 2).start()
        loaded("prompt")
        spread(3, 3)
        loop(1, CHUNKS, lambda chunk: q_copy(chunk, 0, 2).start())
        loaded("sink")
        sink_whole(3, 2).start()
        loaded("kv")
        loop(0, CHUNKS, lambda chunk: own_part(
            chunk,
            lambda head: [pair(sinks, head, 3 * rows_s, 4 * rows_s), pair(kv_ref, head)],
        ))
        spread(3, 2)
        spread_across(3, (3, 2))
        spread(3, 1)
        spread_across(3, (1,))
        spread(3, 0)
        spread_across(3, (0,))
        cross(3)

        def ending(chunk, slots=(0, 1)):
            final(chunk, None, slots, 3)
        ending(0)
        ending(LAST, (0,))
        loop(1, LAST, ending)
        sink_whole(3, 2).wait_send()
        loop(0, CHUNKS, lambda chunk: q_copy(chunk, 0, 2).wait_send())
        drain_prompts(3)


def store_kernel(*refs):
    half = len(refs) // 2
    sems = refs[-1]
    copies = []
    for i in range(half):
        rows = refs[i].shape[0] // STORES
        for j in range(STORES):
            part = slice(j * rows, (j + 1) * rows)
            copies.append(pltpu.make_async_copy(
                refs[i].at[part, :], refs[half + i].at[part, :], sems.at[i, j]
            ))
    for copy in copies:
        copy.start()
    for copy in copies:
        copy.wait()


def self_attention(queries, frame_kv, own_sink, prompts=None):
    rows = queries.shape[0]
    vmem = pl.BlockSpec(memory_space=pltpu.VMEM)
    hbm = pl.BlockSpec(memory_space=pltpu.HBM)
    dma = pltpu.SemaphoreType.DMA
    operands = [queries, frame_kv, own_sink]
    in_specs = [hbm] * 3
    outs = [jax.ShapeDtypeStruct((rows, WIDTH), jnp.bfloat16)]
    scratch = []
    if prompts is not None:
        operands += prompts
        in_specs += [hbm, hbm, pl.BlockSpec(memory_space=pltpu.SMEM)]
        outs = outs * 2
        scratch = [
            pltpu.VMEM((WIN, lax.axis_size("span") // WIN) + prompts[0].shape, jnp.bfloat16),
            pltpu.VMEM((rows, WIDTH), jnp.bfloat16),
            dma((5, WIN)), dma((5, WIN)),
        ]
    results = pl.pallas_call(
        functools.partial(self_kernel, prompts is not None),
        out_shape=[pltpu.VMEM(out.shape, out.dtype) for out in outs],
        in_specs=in_specs,
        out_specs=[vmem] * len(outs),
        scratch_shapes=scratch + [
            pltpu.VMEM((rows, WIDTH), jnp.bfloat16),
            pltpu.VMEM((rows, 2 * WIDTH), jnp.bfloat16),
            pltpu.VMEM((rows, WIDTH), jnp.float32),
            pltpu.VMEM((CHUNKS, rows, 128), jnp.float32),
            dma((5,)),
            pltpu.VMEM((rows, 2 * WIDTH), jnp.bfloat16),
            pltpu.VMEM((WIN * own_sink.shape[0], 2 * WIDTH), jnp.bfloat16),
            pltpu.VMEM((2, rows, WIDTH), jnp.bfloat16),
            pltpu.VMEM((2, rows, WIDTH), jnp.bfloat16),
            pltpu.VMEM((2, rows, WIDTH), jnp.bfloat16),
            pltpu.VMEM((2, CHUNKS, 8, rows), jnp.float32),
            pltpu.VMEM((2, CHUNKS, 8, rows), jnp.float32),
            dma((4, CHUNKS)), dma((4, CHUNKS)),
            dma((2, CHUNKS)), dma((2, CHUNKS)),
            dma((WIN, CHUNKS, 2)), dma((WIN, CHUNKS, 2)),
            dma((2, CHUNKS)), dma((2, CHUNKS)),
            dma((2, CHUNKS)), dma((2, CHUNKS)),
        ],
        compiler_params=pltpu.CompilerParams(
            collective_id=0, has_side_effects=True, vmem_limit_bytes=48 * 1024 * 1024
        ),
    )(*[pltpu.with_memory_space_constraint(x, pltpu.HBM) for x in operands])
    return pl.pallas_call(
        store_kernel,
        out_shape=outs,
        in_specs=[pl.BlockSpec(memory_space=pl.ANY)] * len(outs),
        out_specs=[pl.BlockSpec(memory_space=pl.ANY)] * len(outs),
        scratch_shapes=[dma((len(outs), STORES))],
    )(*[pltpu.with_memory_space_constraint(x, pltpu.VMEM) for x in results])


def cross_kernel(pick_ref, q_ref, k_ref, v_ref, out_ref):
    for inner in range(BUNDLE):
        where = slice(inner * HDIM, (inner + 1) * HDIM)
        blended, _, _ = attend(q_ref[:, where], [(k_ref[0, :, where], v_ref[0, :, where])])
        out_ref[:, where] = blended.astype(jnp.bfloat16)


def cross_attention(cross_queries, prompts, pick):
    rows = cross_queries.shape[0]
    tokens = prompts.shape[1]
    return pl.pallas_call(
        cross_kernel,
        out_shape=jax.ShapeDtypeStruct((rows, WIDTH), jnp.bfloat16),
        grid_spec=pltpu.PrefetchScalarGridSpec(
            num_scalar_prefetch=1,
            grid=(CHUNKS,),
            in_specs=[
                pl.BlockSpec((rows, BW), lambda c, pick: (0, c)),
                pl.BlockSpec((1, tokens, BW), lambda c, pick: (pick[0], 0, c)),
                pl.BlockSpec((1, tokens, BW), lambda c, pick: (pick[0], 0, CHUNKS + c)),
            ],
            out_specs=pl.BlockSpec((rows, BW), lambda c, pick: (0, c)),
        ),
    )(pick.reshape(1), cross_queries, prompts, prompts)


def shards(queries, cross_queries, frame_kv, sink_kv, prompt_kv, switch):
    stream_count = lax.axis_size("span") // WIN
    device = lax.axis_index("span")
    place = device // stream_count
    stream_of = device % stream_count
    own_sink = sink_kv.reshape(sink_kv.shape[1], sink_kv.shape[2])
    if stream_count == 4 and prompt_kv.shape[1] % 16 == 0:
        return tuple(
            self_attention(queries, frame_kv, own_sink, [prompt_kv, cross_queries, switch])
        )
    stream_ids = jnp.arange(switch.shape[0], dtype=jnp.int32)
    switch_at = jnp.sum(jnp.where(stream_ids == stream_of, switch, 0))
    pick = (place >= switch_at).astype(jnp.int32)
    prompts = lax.all_gather(prompt_kv, "span", axis=1, tiled=True)
    (self_out,) = self_attention(queries, frame_kv, own_sink)
    cross_out = cross_attention(cross_queries, prompts, pick)
    return (self_out, cross_out)


def solution(mesh):
    in_specs = (
        P(("groups", "span"), None),
        P(("groups", "span"), None),
        P(("groups", "span"), None),
        P(("groups", "span"), None, None),
        P("groups", "span", None),
        P("groups"),
    )
    out_specs = (P(("groups", "span"), None), P(("groups", "span"), None))
    return jax.shard_map(shards, mesh=mesh, in_specs=in_specs, out_specs=out_specs, check_vma=False)
```

```python
import functools
import math

import jax
import jax.numpy as jnp
from jax import lax
from jax.experimental import pallas as pl
from jax.experimental.pallas import tpu as pltpu
from jax.sharding import PartitionSpec as P

HEADS = 20
HDIM = 128
WIN = 4
BUNDLE = 5
CHUNKS = HEADS // BUNDLE
LAST = CHUNKS - 1
STORES = 1
BW = BUNDLE * HDIM
WIDTH = HEADS * HDIM
SCALE = 1.0 / math.sqrt(HDIM)
LOG2E = 1.4426950408889634
MESH = pl.DeviceIdType.MESH


def attend(query, pieces):
    scores = [
        lax.dot_general(query, keys, (((1,), (1,)), ((), ())), preferred_element_type=jnp.float32)
        for keys, _ in pieces
    ]
    peak = functools.reduce(
        jnp.maximum, [jnp.max(piece, axis=1, keepdims=True) for piece in scores]
    )
    total, blended = None, None
    for piece, (_, values) in zip(scores, pieces):
        weights = jnp.exp2((piece - peak) * (SCALE * LOG2E))
        part_sum = jnp.sum(weights, axis=1, keepdims=True)
        part = jnp.dot(weights.astype(jnp.bfloat16), values, preferred_element_type=jnp.float32)
        total = part_sum if total is None else total + part_sum
        blended = part if blended is None else blended + part
    return blended / total, peak * (SCALE * LOG2E), total


def cols(chunk, width=BW, base=0):
    return pl.ds(pl.multiple_of(base + chunk * width, 128), width)


def head_cols(head, base=0):
    return pl.ds(pl.multiple_of(base + head * HDIM, 128), HDIM)


def self_kernel(with_prompts, *refs):
    if with_prompts:
        (q_hbm, kv_hbm, sink_hbm, prompt_hbm, cq_hbm, pick_ref, out_ref, cross_ref, *refs) = refs
        (bank, cq_ref, pr_s, pr_r, *refs) = refs
    else:
        (q_hbm, kv_hbm, sink_hbm, out_ref, *refs) = refs
    (q_ref, kv_ref, own_out, own_level, load_sem, kv_prev, sinks, q_in, o_send, o_recv, st_send, st_recv,
     kv_s, kv_r, q_s, q_r, s_s, s_r, o_s, o_r, st_s, st_r) = refs
    stride = lax.axis_size("span") // WIN
    me = lax.axis_index("span")
    place = me // stride
    stream = me % stride
    across = (stream + 2) % 4
    beside = stream + 1 - 2 * (stream % 2)
    rows_s = sink_hbm.shape[0]
    rows = q_ref.shape[0]
    mine = pl.ds(pl.multiple_of(place * rows_s, rows_s), rows_s)

    loads = {
        "sink": pltpu.make_async_copy(sink_hbm, sinks.at[mine, :], load_sem.at[0]),
        "q": pltpu.make_async_copy(q_hbm, q_ref, load_sem.at[1]),
        "kv": pltpu.make_async_copy(kv_hbm, kv_ref, load_sem.at[2]),
    }
    if with_prompts:
        loads["prompt"] = pltpu.make_async_copy(
            prompt_hbm, bank.at[place, stream], load_sem.at[3]
        )
        loads["cq"] = pltpu.make_async_copy(cq_hbm, cq_ref, load_sem.at[4])

    def load(*names):
        for name in names:
            if name in loads:
                loads[name].start()

    def loaded(*names):
        for name in names:
            if name in loads:
                loads[name].wait()

    def at_place(index):
        return {"span": index * stride + stream}

    def remote(src, dst, send, recv, index, line=None):
        return pltpu.make_async_remote_copy(
            src_ref=src, dst_ref=dst, send_sem=send, recv_sem=recv,
            device_id=at_place(index) if line is None else {"span": index * stride + line},
            device_id_type=MESH,
        )

    def kv_copies(chunk):
        pairs = []
        for part in range(2):
            where = cols(chunk, BW, part * WIDTH)
            pairs.append((sinks.at[0:rows_s, where], sinks.at[0:rows_s, where]))
        for part in range(2):
            where = cols(chunk, BW, part * WIDTH)
            pairs.append((kv_ref.at[:, where], kv_prev.at[:, where]))
        return [
            remote(src, dst, kv_s.at[i, chunk], kv_r.at[i, chunk], 1)
            for i, (src, dst) in enumerate(pairs)
        ]

    def q_copy(chunk, slot, index):
        return remote(
            q_ref.at[:, cols(chunk)], q_in.at[slot, :, cols(chunk)],
            q_s.at[slot, chunk], q_r.at[slot, chunk], index,
        )

    def q_relay(chunk):
        return remote(
            q_in.at[0, :, cols(chunk)], q_in.at[1, :, cols(chunk)],
            q_s.at[1, chunk], q_r.at[1, chunk], 1,
        )

    def sink_whole(which, index):
        where = sinks.at[which * rows_s : (which + 1) * rows_s, :]
        return remote(where, where, s_s.at[which, 0, 0], s_r.at[which, 0, 0], index)

    def sink_chunk(which, chunk, index):
        copies = []
        for part in range(2):
            where = cols(chunk, BW, part * WIDTH)
            piece = sinks.at[which * rows_s : (which + 1) * rows_s, where]
            copies.append(remote(
                piece, piece, s_s.at[which, chunk, part], s_r.at[which, chunk, part], index
            ))
        return copies

    def lift_copies(frame):
        lane = LAST * (1 - frame)
        copies = []
        for part in range(2):
            where = cols(LAST, BW, part * WIDTH)
            piece = sinks.at[frame * rows_s : (frame + 1) * rows_s, where]
            copies.append(remote(piece, piece, kv_s.at[part, lane], kv_r.at[part, lane], 2))
        for part in range(2):
            where = cols(LAST, BW, part * WIDTH)
            src = (kv_ref if frame else kv_prev).at[:, where]
            dst = kv_prev.at[:, cols(lane, BW, part * WIDTH)]
            copies.append(remote(src, dst, kv_s.at[2 + part, lane], kv_r.at[2 + part, lane], 2))
        return copies

    def o_copy(chunk, slot, index):
        return remote(
            o_send.at[slot, :, cols(chunk)], o_recv.at[slot, :, cols(chunk)],
            o_s.at[slot, chunk], o_r.at[slot, chunk], index,
        )

    def st_copy(chunk, slot, index):
        return remote(
            st_send.at[slot, chunk], st_recv.at[slot, chunk],
            st_s.at[slot, chunk], st_r.at[slot, chunk], index,
        )

    def partial(slot, chunk, pieces_of, index):
        lanes = lax.broadcasted_iota(jnp.int32, (rows, 128), 1)
        stats = jnp.zeros((rows, 128), jnp.float32)
        for inner in range(BUNDLE):
            head = chunk * BUNDLE + inner
            blended, peak, total = attend(q_in[slot, :, head_cols(head)], pieces_of(head))
            o_send[slot, :, head_cols(head)] = blended.astype(jnp.bfloat16)
            stats = jnp.where(lanes == inner, peak + jnp.log2(total), stats)
        st_send[slot, chunk] = jnp.transpose(stats)[0:8]
        o_copy(chunk, slot, index).start()
        st_copy(chunk, slot, index).start()

    def drain_partial(slot, index, chunks):
        def drain(chunk, carry):
            o_copy(chunk, slot, index).wait_send()
            st_copy(chunk, slot, index).wait_send()
            return carry
        lax.fori_loop(0, chunks, drain, 0)

    def own_part(chunk, pieces_of):
        lanes = lax.broadcasted_iota(jnp.int32, (rows, 128), 1)
        stats = jnp.zeros((rows, 128), jnp.float32)
        for inner in range(BUNDLE):
            head = chunk * BUNDLE + inner
            blended, peak, total = attend(q_ref[:, head_cols(head)], pieces_of(head))
            own_out[:, head_cols(head)] = blended
            stats = jnp.where(lanes == inner, peak + jnp.log2(total), stats)
        own_level[chunk] = stats

    def final(chunk, pieces_of, slots, index, own=True):
        levels_in = [own_level[chunk]] if own else []
        for slot in slots:
            o_copy(chunk, slot, index).wait_recv()
            st_copy(chunk, slot, index).wait_recv()
            padded = jnp.concatenate(
                [st_recv[slot, chunk], jnp.zeros((120, rows), jnp.float32)], axis=0
            )
            levels_in.append(jnp.transpose(padded))
        for inner in range(BUNDLE):
            head = chunk * BUNDLE + inner
            where = head_cols(head)
            outs = [own_out[:, where]] if own else []
            outs += [o_recv[slot, :, where].astype(jnp.float32) for slot in slots]
            levels = [level[:, inner : inner + 1] for level in levels_in]
            if pieces_of is not None:
                blended, peak, total = attend(q_ref[:, where], pieces_of(head))
                outs.append(blended)
                levels.append(peak + jnp.log2(total))
            if len(outs) > 1:
                top = functools.reduce(jnp.maximum, levels)
                shares = [jnp.exp2(level - top) for level in levels]
                whole = functools.reduce(jnp.add, shares)
                blended = functools.reduce(
                    jnp.add, [out * share for out, share in zip(outs, shares)]
                ) / whole
            else:
                blended = outs[0]
            out_ref[:, where] = blended.astype(jnp.bfloat16)

    def loop(low, high, body):
        def step(chunk, carry):
            body(chunk)
            return carry
        lax.fori_loop(low, high, step, 0)

    def turn(step):
        return jnp.where(step < 2, step + 1, jnp.where(step < LAST, 0, LAST))

    def pair(ref, head, low=None, high=None):
        part = slice(low, high)
        return ref[part, head_cols(head)], ref[part, head_cols(head, WIDTH)]

    def prompt_copy(kind, piece, line, index, to_line):
        return remote(
            bank.at[piece, line], bank.at[piece, line],
            pr_s.at[kind, piece], pr_r.at[kind if kind > 1 else 0, piece], index, to_line,
        )

    def line_copies(here, piece, kinds=(0, 1, 2, 3)):
        copies = []
        if 0 in kinds and piece <= here < WIN - 1:
            copies.append(prompt_copy(0, piece, stream, here + 1, stream))
        if 1 in kinds and 0 < here <= piece:
            copies.append(prompt_copy(1, piece, stream, here - 1, stream))
        if 2 in kinds:
            copies.append(prompt_copy(2, piece, stream, here, across))
        if 3 in kinds:
            copies.append(prompt_copy(3, piece, stream, here, beside))
        return copies

    def spread(here, piece, kinds=(0, 1, 2, 3)):
        if not with_prompts:
            return
        if piece != here:
            prompt_copy(0, piece, stream, here, stream).wait_recv()
        for copy in line_copies(here, piece, kinds):
            copy.start()

    def spread_across(here, pieces):
        if not with_prompts:
            return
        for piece in pieces:
            prompt_copy(2, piece, across, here, stream).wait_recv()
            prompt_copy(4, piece, across, here, beside).start()

    def cross(here):
        if not with_prompts:
            return
        loaded("cq")
        for piece in range(WIN):
            prompt_copy(3, piece, beside, here, stream).wait_recv()
            prompt_copy(4, piece, 3 - stream, here, stream).wait_recv()
        pick = (place >= pick_ref[stream]).astype(jnp.int32)
        tokens = bank.shape[0] * bank.shape[1] * bank.shape[3]

        def chunk_of(chunk):
            for inner in range(BUNDLE):
                head = chunk * BUNDLE + inner
                keys = bank[:, :, pick, :, head_cols(head)].reshape(tokens, HDIM)
                values = bank[:, :, pick, :, head_cols(head, WIDTH)].reshape(tokens, HDIM)
                blended, _, _ = attend(cq_ref[:, head_cols(head)], [(keys, values)])
                cross_ref[:, head_cols(head)] = blended.astype(jnp.bfloat16)
        loop(0, CHUNKS, chunk_of)

    def drain_prompts(here):
        if not with_prompts:
            return
        for piece in range(WIN):
            for copy in line_copies(here, piece):
                copy.wait_send()
            prompt_copy(4, piece, across, here, beside).wait_send()

    barrier = pltpu.get_barrier_semaphore()
    load("q", "prompt", "sink", "kv", "cq")
    for here, others in enumerate(((1,), (0, 2, 3), (1, 3), (1, 2))):
        @pl.when(place == here)
        def _(others=others):
            for other in others:
                pl.semaphore_signal(
                    barrier, inc=1, device_id=at_place(other), device_id_type=MESH
                )
    if with_prompts:
        for line in (across, beside):
            pl.semaphore_signal(
                barrier, inc=1, device_id={"span": place * stride + line}, device_id_type=MESH
            )

    def greeted(count):
        pl.semaphore_wait(barrier, count + (2 if with_prompts else 0))

    @pl.when(place == 0)
    def _():
        greeted(1)
        loaded("prompt")
        spread(0, 0)
        loaded("sink", "kv")

        def send(chunk):
            for copy in kv_copies(chunk):
                copy.start()
        send(0)
        send(LAST)
        loop(1, LAST, send)
        spread(0, 1)
        spread_across(0, (0, 1))
        loaded("q")
        sink_whole(1, 0).wait_recv()
        loop(0, CHUNKS, lambda chunk: own_part(
            chunk, lambda head: [pair(sinks, head, 0, 2 * rows_s), pair(kv_ref, head)]
        ))
        spread(0, 2)
        spread_across(0, (2,))
        spread(0, 3)
        spread_across(0, (3,))
        cross(0)

        def ending(step):
            chunk = turn(step)
            for which in (2, 3):
                for copy in sink_chunk(which, chunk, 0):
                    copy.wait_recv()
            final(chunk, lambda head: [pair(sinks, head, 2 * rows_s, 4 * rows_s)], (), 0)
        loop(0, CHUNKS, ending)

        def drain(chunk):
            for copy in kv_copies(chunk):
                copy.wait_send()
        loop(0, CHUNKS, drain)
        drain_prompts(0)

    @pl.when(place == 1)
    def _():
        greeted(3)
        loaded("prompt")
        spread(1, 1)
        loaded("sink", "kv")
        for copy in lift_copies(1):
            copy.start()
        sink_whole(1, 0).start()

        def work(chunk):
            for copy in kv_copies(chunk):
                copy.wait_recv()

            def both(slot):
                q_copy(chunk, slot, 1).wait_recv()
                partial(
                    slot, chunk,
                    lambda head: [
                        pair(sinks, head, 0, 2 * rows_s), pair(kv_prev, head), pair(kv_ref, head)
                    ],
                    2 + slot,
                )
            loop(0, 2, both)

        def own(chunk):
            own_part(chunk, lambda head: [
                pair(sinks, head, 0, 2 * rows_s), pair(kv_prev, head), pair(kv_ref, head)
            ])

        def pass_sink(which, chunk):
            for copy in sink_chunk(which, chunk, 1):
                copy.wait_recv()
            for copy in sink_chunk(which, chunk, 0):
                copy.start()

        def lift():
            for copy in kv_copies(LAST):
                copy.wait_recv()
            for copy in lift_copies(0):
                copy.start()

        spread(1, 0)
        spread_across(1, (1, 0))
        loaded("q")

        def early(step):
            chunk = jnp.where(step == 1, LAST, jnp.where(step > 1, step - 1, step))

            @pl.when(step != 1)
            def _():
                work(chunk)

            @pl.when(step == 1)
            def _():
                spread(1, 3)
                lift()

            @pl.when(step == 2)
            def _():
                spread_across(1, (3,))
                loop(2, CHUNKS, lambda piece: pass_sink(2, turn(piece)))
                cross(1)

            @pl.when(step < 2)
            def _():
                own(chunk)

            @pl.when(step == 0)
            def _():
                spread(1, 2)
                spread_across(1, (2,))

            @pl.when(step == 1)
            def _():
                loop(0, 2, lambda piece: pass_sink(2, turn(piece)))
        loop(0, CHUNKS, early)

        def ending(step):
            chunk = turn(step)
            pass_sink(3, chunk)

            @pl.when(step < 2)
            def _():
                final(chunk, lambda head: [
                    pair(sinks, head), pair(kv_prev, head), pair(kv_ref, head)
                ], (), 1, False)

            @pl.when(step >= 2)
            def _():
                final(chunk, lambda head: [pair(sinks, head, 2 * rows_s, 4 * rows_s)], (), 1)
        loop(0, CHUNKS, ending)
        sink_whole(1, 0).wait_send()

        def drain(chunk):
            for which in (2, 3):
                for copy in sink_chunk(which, chunk, 0):
                    copy.wait_send()
        loop(0, CHUNKS, drain)
        for frame in range(2):
            for copy in lift_copies(frame):
                copy.wait_send()
        for slot in range(2):
            drain_partial(slot, 2 + slot, LAST)
        drain_prompts(1)

    @pl.when(place == 2)
    def _():
        greeted(2)

        def send(chunk):
            q_copy(chunk, 0, 1).start()

        def relay(chunk):
            q_copy(chunk, 0, 2).wait_recv()
            q_relay(chunk).start()

        def work(chunk):
            partial(
                0, chunk,
                lambda head: [pair(sinks, head, 2 * rows_s, 3 * rows_s), pair(kv_ref, head)], 3,
            )

        def send_sink(which):
            def body(step):
                for copy in sink_chunk(which, turn(step), 1):
                    copy.start()
            loop(0, CHUNKS, body)

        loaded("q")
        send(0)
        loaded("prompt")
        spread(2, 2)
        relay(0)
        loaded("sink", "kv")
        work(0)
        spread(2, 1)
        spread_across(2, (2, 1))
        spread(2, 3)

        def forward(chunk):
            send(chunk)
            relay(chunk)
        forward(1)
        send_sink(2)
        loop(2, LAST, forward)
        loop(1, LAST, work)
        spread_across(2, (3,))
        spread(2, 0)
        sink_whole(3, 2).wait_recv()
        send_sink(3)
        spread_across(2, (0,))
        loop(0, LAST, lambda chunk: own_part(
            chunk, lambda head: [pair(sinks, head, 2 * rows_s, 4 * rows_s), pair(kv_ref, head)]
        ))
        cross(2)

        def ending(chunk):
            final(chunk, None, (0,), 2)
        ending(0)
        for frame in (1, 0):
            for copy in lift_copies(frame):
                copy.wait_recv()
        q_copy(LAST, 0, 2).wait_recv()

        def lifted(head, high):
            return [
                pair(sinks, head, 0, high), pair(kv_prev, head),
                pair(kv_prev, head - LAST * BUNDLE), pair(kv_ref, head),
            ]
        partial(0, LAST, lambda head: lifted(head, 3 * rows_s), 3)
        final(LAST, lambda head: lifted(head, 4 * rows_s), (), 2, False)
        loop(1, LAST, ending)

        def drain(chunk):
            for which in (2, 3):
                for copy in sink_chunk(which, chunk, 1):
                    copy.wait_send()
        loop(0, CHUNKS, drain)
        loop(0, LAST, lambda chunk: q_copy(chunk, 0, 1).wait_send())
        loop(0, LAST, lambda chunk: q_relay(chunk).wait_send())
        drain_partial(0, 3, CHUNKS)
        drain_prompts(2)

    @pl.when(place == 3)
    def _():
        greeted(2)
        loaded("q")
        q_copy(0, 0, 2).start()
        loaded("prompt")
        spread(3, 3)
        loop(1, CHUNKS, lambda chunk: q_copy(chunk, 0, 2).start())
        loaded("sink")
        sink_whole(3, 2).start()
        loaded("kv")
        loop(0, CHUNKS, lambda chunk: own_part(
            chunk,
            lambda head: [pair(sinks, head, 3 * rows_s, 4 * rows_s), pair(kv_ref, head)],
        ))
        spread(3, 2)
        spread_across(3, (3, 2))
        spread(3, 1)
        spread_across(3, (1,))
        spread(3, 0)
        spread_across(3, (0,))
        cross(3)

        def ending(chunk, slots=(0, 1)):
            final(chunk, None, slots, 3)
        ending(0)
        ending(LAST, (0,))
        loop(1, LAST, ending)
        sink_whole(3, 2).wait_send()
        loop(0, CHUNKS, lambda chunk: q_copy(chunk, 0, 2).wait_send())
        drain_prompts(3)


def store_kernel(*refs):
    half = len(refs) // 2
    sems = refs[-1]
    copies = []
    for i in range(half):
        rows = refs[i].shape[0] // STORES
        for j in range(STORES):
            part = slice(j * rows, (j + 1) * rows)
            copies.append(pltpu.make_async_copy(
                refs[i].at[part, :], refs[half + i].at[part, :], sems.at[i, j]
            ))
    for copy in copies:
        copy.start()
    for copy in copies:
        copy.wait()


def self_attention(queries, frame_kv, own_sink, prompts=None):
    rows = queries.shape[0]
    vmem = pl.BlockSpec(memory_space=pltpu.VMEM)
    hbm = pl.BlockSpec(memory_space=pltpu.HBM)
    dma = pltpu.SemaphoreType.DMA
    operands = [queries, frame_kv, own_sink]
    in_specs = [hbm] * 3
    outs = [jax.ShapeDtypeStruct((rows, WIDTH), jnp.bfloat16)]
    scratch = []
    if prompts is not None:
        operands += prompts
        in_specs += [hbm, hbm, pl.BlockSpec(memory_space=pltpu.SMEM)]
        outs = outs * 2
        scratch = [
            pltpu.VMEM((WIN, lax.axis_size("span") // WIN) + prompts[0].shape, jnp.bfloat16),
            pltpu.VMEM((rows, WIDTH), jnp.bfloat16),
            dma((5, WIN)), dma((5, WIN)),
        ]
    results = pl.pallas_call(
        functools.partial(self_kernel, prompts is not None),
        out_shape=[pltpu.VMEM(out.shape, out.dtype) for out in outs],
        in_specs=in_specs,
        out_specs=[vmem] * len(outs),
        scratch_shapes=scratch + [
            pltpu.VMEM((rows, WIDTH), jnp.bfloat16),
            pltpu.VMEM((rows, 2 * WIDTH), jnp.bfloat16),
            pltpu.VMEM((rows, WIDTH), jnp.float32),
            pltpu.VMEM((CHUNKS, rows, 128), jnp.float32),
            dma((5,)),
            pltpu.VMEM((rows, 2 * WIDTH), jnp.bfloat16),
            pltpu.VMEM((WIN * own_sink.shape[0], 2 * WIDTH), jnp.bfloat16),
            pltpu.VMEM((2, rows, WIDTH), jnp.bfloat16),
            pltpu.VMEM((2, rows, WIDTH), jnp.bfloat16),
            pltpu.VMEM((2, rows, WIDTH), jnp.bfloat16),
            pltpu.VMEM((2, CHUNKS, 8, rows), jnp.float32),
            pltpu.VMEM((2, CHUNKS, 8, rows), jnp.float32),
            dma((4, CHUNKS)), dma((4, CHUNKS)),
            dma((2, CHUNKS)), dma((2, CHUNKS)),
            dma((WIN, CHUNKS, 2)), dma((WIN, CHUNKS, 2)),
            dma((2, CHUNKS)), dma((2, CHUNKS)),
            dma((2, CHUNKS)), dma((2, CHUNKS)),
        ],
        compiler_params=pltpu.CompilerParams(
            collective_id=0, has_side_effects=True, vmem_limit_bytes=48 * 1024 * 1024
        ),
    )(*[pltpu.with_memory_space_constraint(x, pltpu.HBM) for x in operands])
    return pl.pallas_call(
        store_kernel,
        out_shape=outs,
        in_specs=[pl.BlockSpec(memory_space=pl.ANY)] * len(outs),
        out_specs=[pl.BlockSpec(memory_space=pl.ANY)] * len(outs),
        scratch_shapes=[dma((len(outs), STORES))],
    )(*[pltpu.with_memory_space_constraint(x, pltpu.VMEM) for x in results])


def cross_kernel(pick_ref, q_ref, k_ref, v_ref, out_ref):
    for inner in range(BUNDLE):
        where = slice(inner * HDIM, (inner + 1) * HDIM)
        blended, _, _ = attend(q_ref[:, where], [(k_ref[0, :, where], v_ref[0, :, where])])
        out_ref[:, where] = blended.astype(jnp.bfloat16)


def cross_attention(cross_queries, prompts, pick):
    rows = cross_queries.shape[0]
    tokens = prompts.shape[1]
    return pl.pallas_call(
        cross_kernel,
        out_shape=jax.ShapeDtypeStruct((rows, WIDTH), jnp.bfloat16),
        grid_spec=pltpu.PrefetchScalarGridSpec(
            num_scalar_prefetch=1,
            grid=(CHUNKS,),
            in_specs=[
                pl.BlockSpec((rows, BW), lambda c, pick: (0, c)),
                pl.BlockSpec((1, tokens, BW), lambda c, pick: (pick[0], 0, c)),
                pl.BlockSpec((1, tokens, BW), lambda c, pick: (pick[0], 0, CHUNKS + c)),
            ],
            out_specs=pl.BlockSpec((rows, BW), lambda c, pick: (0, c)),
        ),
    )(pick.reshape(1), cross_queries, prompts, prompts)


def shards(queries, cross_queries, frame_kv, sink_kv, prompt_kv, switch):
    stream_count = lax.axis_size("span") // WIN
    device = lax.axis_index("span")
    place = device // stream_count
    stream_of = device % stream_count
    own_sink = sink_kv.reshape(sink_kv.shape[1], sink_kv.shape[2])
    if stream_count == 4 and prompt_kv.shape[1] % 16 == 0:
        return tuple(
            self_attention(queries, frame_kv, own_sink, [prompt_kv, cross_queries, switch])
        )
    stream_ids = jnp.arange(switch.shape[0], dtype=jnp.int32)
    switch_at = jnp.sum(jnp.where(stream_ids == stream_of, switch, 0))
    pick = (place >= switch_at).astype(jnp.int32)
    prompts = lax.all_gather(prompt_kv, "span", axis=1, tiled=True)
    (self_out,) = self_attention(queries, frame_kv, own_sink)
    cross_out = cross_attention(cross_queries, prompts, pick)
    return (self_out, cross_out)


def solution(mesh):
    in_specs = (
        P(("groups", "span"), None),
        P(("groups", "span"), None),
        P(("groups", "span"), None),
        P(("groups", "span"), None, None),
        P("groups", "span", None),
        P("groups"),
    )
    out_specs = (P(("groups", "span"), None), P(("groups", "span"), None))
    return jax.shard_map(shards, mesh=mesh, in_specs=in_specs, out_specs=out_specs, check_vma=False)
```
